32 devices in a mesh: gx: 4 (over z), gy: 8 (over y, x, core).
Axes of the slice: x: 2, y: 2, z: 4, core: 2. Of those that a mesh axis runs over, the one named last changes fastest.
Arguments:
- features: bfloat16 [8192, 512], P(('gx', 'gy')), may hold values from -6 to 6
- cotangent: bfloat16 [8192, 512], P(('gx', 'gy')), may hold values from -6 to 6
- self_weight: bfloat16 [3, 512, 512], replicated, may hold values from -0.25 to 0.25
- neigh_weight: bfloat16 [3, 512, 512], replicated, may hold values from -0.25 to 0.25
- block_val: bfloat16 [64, 4, 128, 128], P(('gx', 'gy')), may hold values from -0.25 to 0.25
- block_col: int32 [64, 4], P(('gx', 'gy')), may hold values from 0 to 5
- send_idx: int32 [32, 32, 16], P(('gx', 'gy')), may hold values from 0 to 255
- send_count: int32 [32, 32], P(('gx', 'gy')), may hold values from 0 to 16, as said below
Outputs:
- self_grad: bfloat16 [3, 512, 512], replicated
- neigh_grad: bfloat16 [3, 512, 512], replicated
- input_grad: bfloat16 [8192, 512], P(('gx', 'gy'))
The draws below stay inside these ranges and needn't reach their ends.
Inputs may be any that keep to these rules, and one draw needn't show every extreme that they name: `send_count`: at most 16 rows from one device to one peer; in every draw some receivers get exactly 16 from every device.
All inputs are finite; a program needn't handle non-finite values.
Results may differ from the reference program's by a relative error of at most 0.02.
Values may be sent and summed in bfloat16 or wider, within the bound.
No kernel may reach another device: no remote copies, remote signals or barrier semaphores. Data moves between devices by JAX's collectives and lax.ppermute only.
A program may use at most 128 MiB of HBM per device.

```python
import math
import jax
import jax.numpy as jnp
from jax import lax

D = 512
TILE = 128
BPT = 4
LAYERS = 3
NODE_DEV = 256
HALO_DEV = 512
SLOT = 16
NODES = 8192
TILES_DEV = 2
EXT_TILES = 6
DEVICES = 32


def draw_send_count(key, part):
    base_key, hot_key = jax.random.split(jax.random.fold_in(key, 11))
    counts = jax.random.randint(base_key, (DEVICES, DEVICES), 0, SLOT + 1)
    ranks = jax.random.permutation(hot_key, DEVICES)
    hotset = ranks < max(DEVICES // 8, 1)
    return jnp.where(hotset[None, :], SLOT, counts).astype(jnp.int32)


def place_ends(result, rng, low, top_value):
    shape = result.shape
    place = [jax.random.randint(jax.random.fold_in(rng, axis), (), 0, shape[axis]) for axis in range(len(shape))]
    result = result.at[tuple(place)].set(low)
    longest = shape.index(max(shape))
    place[longest] = (place[longest] + 1) % shape[longest]
    return result.at[tuple(place)].set(top_value)


def spiked(drawn, key, source, target, parts, factor):
    def block_of(dim):
        return (jnp.arange(drawn.shape[dim]) // (drawn.shape[dim] // parts)).reshape((-1,) + (1,) * (drawn.ndim - 1 - dim))

    near = jax.random.permutation(key, parts)[block_of(target)]
    second = (block_of(target) + parts // 2) % parts
    return jnp.where((block_of(source) == near) | (block_of(source) == second), factor * drawn, drawn)


def shard_levels(stream_key, dims, cuts, least, largest):
    level, own = 1.0, jax.random.fold_in(stream_key, 6)
    for position, shards_of in cuts:
        draws = jnp.exp(jax.random.uniform(jax.random.fold_in(own, position), (shards_of,), jnp.float32, least / len(cuts), largest / len(cuts)))
        level = level * jnp.repeat(draws, dims[position] // shards_of).reshape([-1 if axis == position else 1 for axis in range(len(dims))])
    return level


def scatter_about(own_key, dims, scale, most, pieces=(), held_as=jnp.bfloat16):
    loudness = shard_levels(own_key, dims, pieces, -0.22, 0.18) if pieces else 1.0
    result = jax.random.normal(own_key, dims, jnp.float32) * scale * loudness
    return jnp.minimum(jnp.maximum(result, -most), most).astype(held_as)


def bell_draw_with(own_key, dims, deviation, most, cuts, heavy, kind=jnp.bfloat16):
    array = deviation * jax.random.normal(own_key, dims, jnp.float32)
    if cuts:
        array = array * shard_levels(own_key, dims, cuts, -0.22, 0.18)
    return jnp.clip(spiked(array, jax.random.fold_in(own_key, 3), *heavy), -most, most).astype(kind)


def setup_inputs(seed: int = 0) -> dict:
    arg_keys = jax.random.split(jax.random.key(seed), 9)
    return {
        "features": bell_draw_with(arg_keys[0], (NODES, D), 1.0, 6.0, ((0, 32),), (0, 1, 32, 2.75)),
        "cotangent": bell_draw_with(arg_keys[1], (NODES, D), 1.0, 6.0, ((0, 32),), (0, 1, 32, 2.75)),
        "self_weight": scatter_about(arg_keys[2], (LAYERS, D, D), D ** -0.5, 0.25),
        "neigh_weight": scatter_about(arg_keys[3], (LAYERS, D, D), D ** -0.5, 0.25),
        "block_val": scatter_about(arg_keys[4], (DEVICES * TILES_DEV, BPT, TILE, TILE), (BPT * TILE) ** -0.5, 0.25, ((0, 32),)),
        "block_col": place_ends(jax.random.randint(arg_keys[5], (DEVICES * TILES_DEV, BPT), 0, EXT_TILES), jax.random.fold_in(arg_keys[5], 1), 0, EXT_TILES - 1).astype(jnp.int32),
        "send_idx": place_ends(jax.random.randint(arg_keys[6], (DEVICES, DEVICES, SLOT), 0, NODE_DEV), jax.random.fold_in(arg_keys[6], 1), 0, NODE_DEV - 1).astype(jnp.int32),
        "send_count": draw_send_count(jax.random.fold_in(arg_keys[8], 71), 0),
    }


def reference(features, cotangent, self_weight, neigh_weight, block_val, block_col, send_idx, send_count):
    tiles_dev = NODE_DEV // TILE
    ext_tiles = (NODE_DEV + HALO_DEV) // TILE
    owners = (jnp.arange(DEVICES, dtype=jnp.int32)[:, None, None] * NODE_DEV + send_idx.astype(jnp.int32)).reshape(-1)
    live = (jnp.arange(SLOT, dtype=jnp.int32)[None, None, :] < send_count[:, :, None]).reshape(-1, 1)
    values = block_val.reshape(DEVICES, tiles_dev, BPT, TILE, TILE)
    columns = block_col.reshape(DEVICES, tiles_dev, BPT)
    scale = 1.0 / math.sqrt(NODES)

    def boundary(hidden):
        picked = jnp.where(live, hidden[owners], jnp.zeros((), hidden.dtype))
        picked = picked.reshape(DEVICES, DEVICES, SLOT, D).transpose(1, 0, 2, 3)
        return picked.reshape(DEVICES, HALO_DEV, D)

    def gather_sum(items):
        extended, vals, cols = items
        tiled = extended.reshape(ext_tiles, TILE, D)[cols]
        total = jnp.einsum('rbij,rbjd->rid', vals.astype(jnp.float32), tiled.astype(jnp.float32))
        return total.reshape(NODE_DEV, D)

    def spread(items):
        upstream, vals, cols = items
        contrib = jnp.einsum('rbij,rid->rbjd', vals.astype(jnp.float32), upstream.reshape(tiles_dev, TILE, D).astype(jnp.float32))
        total = jnp.zeros((ext_tiles, TILE, D), jnp.float32).at[cols.reshape(-1)].add(contrib.reshape(-1, TILE, D))
        return total.reshape(NODE_DEV + HALO_DEV, D)
    hiddens = [features]
    aggregates = []
    preacts = []
    hidden = features
    for layer_at in range(LAYERS):
        extended = jnp.concatenate([hidden.reshape(DEVICES, NODE_DEV, D), boundary(hidden)], axis=1)
        aggregate = lax.map(gather_sum, (extended, values, columns)).reshape(NODES, D).astype(jnp.bfloat16)
        preact = jnp.dot(hidden, self_weight[layer_at], preferred_element_type=jnp.float32) + jnp.dot(aggregate, neigh_weight[layer_at], preferred_element_type=jnp.float32)
        aggregates.append(aggregate)
        preacts.append(preact)
        if layer_at < LAYERS - 1:
            hidden = jax.nn.silu(preact).astype(jnp.bfloat16)
            hiddens.append(hidden)
    self_list = [None] * LAYERS
    neigh_list = [None] * LAYERS
    grad = cotangent
    for layer_at in reversed(range(LAYERS)):
        preact = preacts[layer_at]
        sigma = jax.nn.sigmoid(preact)
        delta = (grad.astype(jnp.float32) * sigma * (1.0 + preact * (1.0 - sigma))).astype(jnp.bfloat16)
        self_list[layer_at] = (jnp.dot(hiddens[layer_at].T, delta, preferred_element_type=jnp.float32) * scale).astype(jnp.bfloat16)
        neigh_list[layer_at] = (jnp.dot(aggregates[layer_at].T, delta, preferred_element_type=jnp.float32) * scale).astype(jnp.bfloat16)
        own_part = jnp.dot(delta, self_weight[layer_at].T, preferred_element_type=jnp.float32)
        upstream = jnp.dot(delta, neigh_weight[layer_at].T, preferred_element_type=jnp.float32).astype(jnp.bfloat16)
        ext_grad = lax.map(spread, (upstream.reshape(DEVICES, NODE_DEV, D), values, columns))
        halo_grad = ext_grad[:, NODE_DEV:].astype(jnp.bfloat16).reshape(DEVICES, DEVICES, SLOT, D)
        halo_grad = halo_grad.transpose(1, 0, 2, 3).reshape(-1, D)
        returned = jnp.zeros((NODES, D), jnp.float32).at[owners].add(jnp.where(live, halo_grad.astype(jnp.float32), jnp.zeros((), jnp.float32)))
        grad = (own_part + ext_grad[:, :NODE_DEV].reshape(NODES, D) + returned).astype(jnp.bfloat16)
    return (jnp.stack(self_list), jnp.stack(neigh_list), grad)
```

```python
import functools
import math

import jax
import jax.numpy as jnp
from jax import lax
from jax.experimental import pallas as pl
from jax.experimental.pallas import tpu as pltpu
from jax.sharding import PartitionSpec as P

AXES = ("gx", "gy")
VMEM = pl.BlockSpec(memory_space=pltpu.VMEM)
SMEM = pl.BlockSpec(memory_space=pltpu.SMEM)


def mm(a, b):
    return jnp.dot(a, b, preferred_element_type=jnp.float32)


def mm_tn(a, b):
    return lax.dot_general(a, b, (((0,), (0,)), ((), ())), preferred_element_type=jnp.float32)


def mm_nt(a, b):
    return lax.dot_general(a, b, (((1,), (1,)), ((), ())), preferred_element_type=jnp.float32)


def iota(shape, dim):
    return lax.broadcasted_iota(jnp.int32, shape, dim)


def ones_where(mask):
    return jnp.where(mask, 1.0, 0.0).astype(jnp.bfloat16)


def pick_rows(col, table):
    hot = ones_where(iota((col.shape[0], table.shape[0]), 1) == col)
    return mm(hot, table).astype(jnp.bfloat16)


def return_rows(row, arrived, nodes):
    hot = ones_where(iota((nodes, row.shape[1]), 0) == row)
    return mm(hot, arrived)


def first_kernel(idx_ref, cnt_ref, x_ref, row_ref, col_ref, send_ref):
    peers, slots = idx_ref.shape
    total = peers * slots
    eye = iota((peers, peers), 0) == iota((peers, peers), 1)
    counts = jnp.broadcast_to(cnt_ref[...].astype(jnp.float32), (peers, peers))
    count_col = jnp.sum(jnp.where(eye, counts, 0.0), axis=1, keepdims=True)
    live = iota((peers, slots), 1).astype(jnp.float32) < count_col
    code = jnp.where(live, idx_ref[...].astype(jnp.float32) + 1.0, 0.0).astype(jnp.bfloat16)
    spread = ones_where((iota((slots, total), 1) & (slots - 1)) == iota((slots, total), 0))
    start = iota((peers, total), 0) * slots
    place = iota((peers, total), 1)
    inside = (place >= start) & (place < start + slots)
    row = jnp.sum(jnp.where(inside, mm(code, spread), 0.0), axis=0, keepdims=True) - 1.0
    row_ref[...] = row.astype(jnp.int32)
    start_t = iota((total, peers), 1) * slots
    place_t = iota((total, peers), 0)
    inside_t = ones_where((place_t >= start_t) & (place_t < start_t + slots))
    here = (iota((total, slots), 0) & (slots - 1)) == iota((total, slots), 1)
    col = jnp.sum(jnp.where(here, mm(inside_t, code), 0.0), axis=1, keepdims=True) - 1.0
    col = col.astype(jnp.int32)
    col_ref[...] = col
    send_ref[...] = pick_rows(col, x_ref[...])


def aggregate_into(agg_ref, ext_ref, cols_ref, hid_ref, arr_ref, val_ref):
    tiles, blocks, tile, _ = val_ref.shape
    own = hid_ref.shape[0] // tile
    for t in range(own):
        ext_ref[t] = hid_ref[t * tile : (t + 1) * tile, :]
    for t in range(arr_ref.shape[0] // tile):
        ext_ref[own + t] = arr_ref[t * tile : (t + 1) * tile, :]
    for r in range(tiles):
        total = mm(val_ref[r, 0], ext_ref[cols_ref[r, 0]])
        for b in range(1, blocks):
            total += mm(val_ref[r, b], ext_ref[cols_ref[r, b]])
        agg_ref[r * tile : (r + 1) * tile, :] = total.astype(jnp.bfloat16)


def pre_and_sigma(agg_ref, hid_ref, ws_ref, wn_ref):
    pre = mm(hid_ref[...], ws_ref[0]) + mm(agg_ref[...], wn_ref[0])
    return pre, jax.nn.sigmoid(pre)


def middle_kernel(
    cols_ref, hid_ref, arr_ref, val_ref, ws_ref, wn_ref, col_ref,
    agg_ref, slope_ref, next_ref, send_ref, ext_ref,
):
    aggregate_into(agg_ref, ext_ref, cols_ref, hid_ref, arr_ref, val_ref)
    pre, sigma = pre_and_sigma(agg_ref, hid_ref, ws_ref, wn_ref)
    hidden = (pre * sigma).astype(jnp.bfloat16)
    next_ref[...] = hidden
    send_ref[...] = pick_rows(col_ref[...], hidden)
    slope_ref[...] = sigma * (1.0 + pre * (1.0 - sigma))


def spread_back(delta, cols_ref, val_ref, ws_ref, wn_ref, halo_ref, base_ref, acc_ref):
    tiles, blocks, tile, _ = val_ref.shape
    own = base_ref.shape[0] // tile
    acc_ref[...] = jnp.zeros_like(acc_ref)
    upstream = mm_nt(delta, wn_ref[0]).astype(jnp.bfloat16)
    for r in range(tiles):
        part = upstream[r * tile : (r + 1) * tile, :]
        for b in range(blocks):
            c = cols_ref[r, b]
            acc_ref[c] += mm_tn(val_ref[r, b], part)
    for t in range(halo_ref.shape[0] // tile):
        halo_ref[t * tile : (t + 1) * tile, :] = acc_ref[own + t].astype(jnp.bfloat16)
    own_part = mm_nt(delta, ws_ref[0])
    for t in range(own):
        rows = slice(t * tile, (t + 1) * tile)
        base_ref[rows, :] = own_part[rows, :] + acc_ref[t]


def last_kernel(
    cols_ref, hid_ref, arr_ref, val_ref, ws_ref, wn_ref, cot_ref,
    agg_ref, delta_ref, halo_ref, base_ref, ext_ref, acc_ref,
):
    aggregate_into(agg_ref, ext_ref, cols_ref, hid_ref, arr_ref, val_ref)
    pre, sigma = pre_and_sigma(agg_ref, hid_ref, ws_ref, wn_ref)
    slope = sigma * (1.0 + pre * (1.0 - sigma))
    delta = (cot_ref[...].astype(jnp.float32) * slope).astype(jnp.bfloat16)
    delta_ref[...] = delta
    spread_back(delta, cols_ref, val_ref, ws_ref, wn_ref, halo_ref, base_ref, acc_ref)


def backward_kernel(
    cols_ref, arr_ref, before_ref, slope_ref, row_ref, val_ref, ws_ref, wn_ref,
    delta_ref, halo_ref, base_ref, acc_ref,
):
    back = return_rows(row_ref[...], arr_ref[...], before_ref.shape[0])
    grad = (before_ref[...] + back).astype(jnp.bfloat16)
    delta = (grad.astype(jnp.float32) * slope_ref[...]).astype(jnp.bfloat16)
    delta_ref[...] = delta
    spread_back(delta, cols_ref, val_ref, ws_ref, wn_ref, halo_ref, base_ref, acc_ref)


def final_kernel(arr_ref, before_ref, row_ref, out_ref):
    back = return_rows(row_ref[...], arr_ref[...], before_ref.shape[0])
    out_ref[...] = (before_ref[...] + back).astype(jnp.bfloat16)


def weight_kernel(core_ref, hid_ref, agg_ref, delta_ref, keep_ref, give_ref):
    delta = delta_ref[...]

    @pl.when(core_ref[0] == 0)
    def _():
        keep_ref[...] = mm_tn(hid_ref[...], delta)
        give_ref[...] = mm_tn(agg_ref[...], delta).astype(jnp.bfloat16)

    @pl.when(core_ref[0] != 0)
    def _():
        keep_ref[...] = mm_tn(agg_ref[...], delta)
        give_ref[...] = mm_tn(hid_ref[...], delta).astype(jnp.bfloat16)


def per_device(
    features, cotangent, self_weight, neigh_weight, block_val, block_col, send_idx, send_count
):
    outer = lax.axis_size("gx")
    inner = lax.axis_size("gy")
    devices = outer * inner
    nodes, width = features.shape
    tile = block_val.shape[2]
    layers = self_weight.shape[0]
    slots = send_idx.shape[2]
    halo = devices * slots
    ext_tiles = (nodes + halo) // tile
    scale = 1.0 / math.sqrt(nodes * devices)
    bf16, f32 = jnp.bfloat16, jnp.float32

    def shape(rows, dtype):
        return jax.ShapeDtypeStruct((rows, width), dtype)

    def layer_spec(layer):
        return pl.BlockSpec((1, width, width), lambda i, layer=layer: (layer, 0, 0))

    def whole(array):
        return pl.BlockSpec(array.shape, lambda i, n=array.ndim: (0,) * n)

    def call(body, name, args, outs, scratch=(), layer=None, flops=0):
        specs = []
        for array in args:
            if array is block_col or array.ndim == 1:
                specs.append(SMEM)
            elif array is self_weight or array is neigh_weight:
                specs.append(layer_spec(layer))
            else:
                specs.append(whole(array))
        moved = sum(math.prod(o.shape) * o.dtype.itemsize for o in outs)
        return pl.pallas_call(
            body,
            grid=(1,),
            name=name,
            in_specs=specs,
            out_specs=[whole(o) for o in outs],
            out_shape=list(outs),
            scratch_shapes=list(scratch),
            cost_estimate=pl.CostEstimate(
                flops=flops, bytes_accessed=2 * moved, transcendentals=0
            ),
            compiler_params=pltpu.CompilerParams(vmem_limit_bytes=24 << 20),
        )(*args)

    def exchange(rows):
        blocks = rows.reshape(devices, slots, width)
        return lax.all_to_all(blocks, AXES, 0, 0, tiled=True).reshape(halo, width)

    position = lax.axis_index("gy")
    core = position & 1
    core_arg = core.reshape(1)
    ext_scratch = pltpu.VMEM((ext_tiles, tile, width), bf16)
    acc_scratch = pltpu.VMEM((ext_tiles, tile, width), f32)
    big = 8 * nodes * width * width

    bits = list(range(1, inner.bit_length() - 1))
    turn = bits[len(bits) // 2 :] + bits[: len(bits) // 2]
    gx_bits = list(range(outer.bit_length() - 1))

    def flip(array, even, odd):
        perm = [(j, j ^ (1 << (odd if j & 1 else even))) for j in range(inner)]
        return lax.ppermute(array, "gy", perm)

    def side(even, odd):
        return jnp.where(core == 0, (position >> even) & 1, (position >> odd) & 1)

    def reduce_all(keep, give):
        total = keep + flip(give, 0, 0).astype(f32)
        for even, odd in zip(bits, turn):
            half = total.shape[0] // 2
            b = side(even, odd)
            mine = lax.dynamic_slice(total, (b * half, 0), (half, width))
            theirs = lax.dynamic_slice(total, ((1 - b) * half, 0), (half, width))
            total = mine + flip(theirs.astype(bf16), even, odd).astype(f32)
        for bit in gx_bits:
            mine = total.astype(bf16)
            perm = [(j, j ^ (1 << bit)) for j in range(outer)]
            total = mine.astype(f32) + lax.ppermute(mine, "gx", perm).astype(f32)
        piece = (total * scale).astype(bf16)
        for even, odd in zip(bits[::-1], turn[::-1]):
            b = side(even, odd)
            got = flip(piece, even, odd)
            piece = jnp.where(
                b == 0, jnp.concatenate([piece, got]), jnp.concatenate([got, piece])
            )
        other = flip(piece, 0, 0)
        return jnp.where(core == 0, piece, other), jnp.where(core == 0, other, piece)

    row, col, send = call(
        first_kernel,
        "first",
        (send_idx.reshape(devices, slots), send_count, features),
        (
            jax.ShapeDtypeStruct((1, halo), jnp.int32),
            jax.ShapeDtypeStruct((halo, 1), jnp.int32),
            shape(halo, bf16),
        ),
    )
    hiddens, aggregates, slopes, deltas = [features], [], [], [None] * layers
    hidden = features
    for layer in range(layers - 1):
        arrived = exchange(send)
        aggregate, slope, hidden, send = call(
            middle_kernel,
            f"forward{layer}",
            (block_col, hidden, arrived, block_val, self_weight, neigh_weight, col),
            (shape(nodes, bf16), shape(nodes, f32), shape(nodes, bf16), shape(halo, bf16)),
            (ext_scratch,),
            layer,
            big,
        )
        hiddens.append(hidden)
        aggregates.append(aggregate)
        slopes.append(slope)
    arrived = exchange(send)
    aggregate, delta, outgoing, base = call(
        last_kernel,
        "turn",
        (block_col, hidden, arrived, block_val, self_weight, neigh_weight, cotangent),
        (shape(nodes, bf16), shape(nodes, bf16), shape(halo, bf16), shape(nodes, f32)),
        (ext_scratch, acc_scratch),
        layers - 1,
        2 * big,
    )
    aggregates.append(aggregate)
    self_list, neigh_list = [None] * layers, [None] * layers
    for layer in reversed(range(layers)):
        keep, give = call(
            weight_kernel,
            f"weight{layer}",
            (core_arg, hiddens[layer], aggregates[layer], delta),
            (shape(width, f32), shape(width, bf16)),
            flops=4 * nodes * width * width,
        )
        self_list[layer], neigh_list[layer] = reduce_all(keep, give)
        arrived = exchange(outgoing)
        if layer:
            delta, outgoing, base = call(
                backward_kernel,
                f"backward{layer - 1}",
                (block_col, arrived, base, slopes[layer - 1], row, block_val)
                + (self_weight, neigh_weight),
                (shape(nodes, bf16), shape(halo, bf16), shape(nodes, f32)),
                (acc_scratch,),
                layer - 1,
                big,
            )
    (grad,) = call(final_kernel, "final", (arrived, base, row), (shape(nodes, bf16),))
    return jnp.stack(self_list), jnp.stack(neigh_list), grad


def solution(mesh):
    return jax.shard_map(
        per_device,
        mesh=mesh,
        in_specs=(
            P(AXES, None),
            P(AXES, None),
            P(),
            P(),
            P(AXES, None, None, None),
            P(AXES, None),
            P(AXES, None, None),
            P(AXES, None),
        ),
        out_specs=(P(), P(), P(AXES, None)),
        check_vma=False,
    )
```

```python
import functools
import math

import jax
import jax.numpy as jnp
from jax import lax
from jax.experimental import pallas as pl
from jax.experimental.pallas import tpu as pltpu
from jax.sharding import PartitionSpec as P


AXES = ("gx", "gy")
SMEM = pl.BlockSpec(memory_space=pltpu.SMEM)
HBM = pl.BlockSpec(memory_space=pltpu.HBM)
ANY = pl.BlockSpec(memory_space=pl.ANY)


def mm(a, b):
    return jnp.dot(a, b, preferred_element_type=jnp.float32)


def mm_tn(a, b):
    return lax.dot_general(a, b, (((0,), (0,)), ((), ())), preferred_element_type=jnp.float32)


def mm_nt(a, b):
    return lax.dot_general(a, b, (((1,), (1,)), ((), ())), preferred_element_type=jnp.float32)


def iota(shape, dim):
    return lax.broadcasted_iota(jnp.int32, shape, dim)


def ones_where(mask):
    return jnp.where(mask, 1.0, 0.0).astype(jnp.bfloat16)


def pick_rows(col, table):
    hot = ones_where(iota((col.shape[0], table.shape[0]), 1) == col)
    return mm(hot, table).astype(jnp.bfloat16)


def return_rows(row, arrived, nodes):
    hot = ones_where(iota((nodes, row.shape[1]), 0) == row)
    return mm(hot, arrived)


class Copies:
    def __init__(self, sems):
        self.sems, self.used, self.stores = sems, 0, []

    def start(self, source, target):
        copy = pltpu.make_async_copy(source, target, self.sems.at[self.used])
        self.used += 1
        copy.start()
        return copy

    def store(self, source, target):
        self.stores.append(self.start(source, target))

    def finish(self):
        for copy in self.stores:
            copy.wait()


def first_kernel(idx, cnt, x, row_out, col_out, send_out, idx_v, cnt_v, x_v, row_v, col_v, send_v, sems):
    go = Copies(sems)
    loads = [go.start(idx, idx_v), go.start(cnt, cnt_v), go.start(x, x_v)]
    for load in loads[:2]:
        load.wait()
    _, peers, slots = idx.shape
    total = peers * slots
    eye = iota((peers, peers), 0) == iota((peers, peers), 1)
    counts = jnp.broadcast_to(cnt_v[...].astype(jnp.float32), (peers, peers))
    count_col = jnp.sum(jnp.where(eye, counts, 0.0), axis=1, keepdims=True)
    live = iota((peers, slots), 1).astype(jnp.float32) < count_col
    code = jnp.where(live, idx_v[0].astype(jnp.float32) + 1.0, 0.0).astype(jnp.bfloat16)
    start_t = iota((total, peers), 1) * slots
    place_t = iota((total, peers), 0)
    inside_t = ones_where((place_t >= start_t) & (place_t < start_t + slots))
    here = (iota((total, slots), 0) & (slots - 1)) == iota((total, slots), 1)
    col = jnp.sum(jnp.where(here, mm(inside_t, code), 0.0), axis=1, keepdims=True) - 1.0
    col = col.astype(jnp.int32)
    col_v[...] = col
    go.store(col_v, col_out)
    spread = ones_where((iota((slots, total), 1) & (slots - 1)) == iota((slots, total), 0))
    start = iota((peers, total), 0) * slots
    place = iota((peers, total), 1)
    inside = (place >= start) & (place < start + slots)
    row = jnp.sum(jnp.where(inside, mm(code, spread), 0.0), axis=0, keepdims=True) - 1.0
    row_v[...] = row.astype(jnp.int32)
    go.store(row_v, row_out)
    loads[2].wait()
    send_v[...] = pick_rows(col, x_v[...])
    go.store(send_v, send_out)
    go.finish()


def aggregate_into(agg_v, ext_v, cols, val_v):
    tiles, blocks, tile, _ = val_v.shape
    for r in range(tiles):
        total = mm(val_v[r, 0], ext_v[cols[r, 0]])
        for b in range(1, blocks):
            total += mm(val_v[r, b], ext_v[cols[r, b]])
        agg_v[r * tile : (r + 1) * tile, :] = total.astype(jnp.bfloat16)


def own_rows(ext_v, own):
    return ext_v[:own].reshape(own * ext_v.shape[1], ext_v.shape[2])


def forward_loads(go, layer, hid, arr, val, ws, wn, ext_v, val_v, ws_v, wn_v):
    own = hid.shape[0]
    return [
        go.start(hid, ext_v.at[pl.ds(0, own)]),
        go.start(ws.at[layer], ws_v),
        go.start(arr, ext_v.at[pl.ds(own, arr.shape[0])]),
        go.start(val, val_v),
        go.start(wn.at[layer], wn_v),
    ]


def pre_activation(loads, cols, own, ext_v, val_v, ws_v, wn_v, agg_v):
    loads[0].wait()
    loads[1].wait()
    pre = mm(own_rows(ext_v, own), ws_v[...])
    loads[2].wait()
    loads[3].wait()
    aggregate_into(agg_v, ext_v, cols, val_v)
    loads[4].wait()
    return pre + mm(agg_v[...], wn_v[...])


def middle_kernel(
    layer, cols, hid, arr, val, ws, wn, col, agg_out, slope_out, next_out, send_out,
    ext_v, val_v, ws_v, wn_v, col_v, agg_v, slope_v, next_v, send_v, sems,
):
    go = Copies(sems)
    loads = forward_loads(go, layer, hid, arr, val, ws, wn, ext_v, val_v, ws_v, wn_v)
    col_load = go.start(col, col_v)
    pre = pre_activation(loads, cols, hid.shape[0], ext_v, val_v, ws_v, wn_v, agg_v)
    go.store(agg_v, agg_out)
    sigma = jax.nn.sigmoid(pre)
    hidden = (pre * sigma).astype(jnp.bfloat16)
    next_v[...] = hidden
    go.store(next_v, next_out)
    slope_v[...] = sigma * (1.0 + pre * (1.0 - sigma))
    go.store(slope_v, slope_out)
    col_load.wait()
    send_v[...] = pick_rows(col_v[...], hidden)
    go.store(send_v, send_out)
    go.finish()


def spread_back(go, delta, cols, val_v, ws_v, wn_load, wn_v, halo_out, base_out, halo_v, base_v, acc_v):
    tiles, blocks, tile, _ = val_v.shape
    own = tiles
    acc_v[...] = jnp.zeros_like(acc_v)
    if wn_load is not None:
        wn_load.wait()
    upstream = mm_nt(delta, wn_v[...]).astype(jnp.bfloat16)
    for r in range(tiles):
        part = upstream[r * tile : (r + 1) * tile, :]
        for b in range(blocks):
            c = cols[r, b]
            acc_v[c] += mm_tn(val_v[r, b], part)
    halo_v[...] = acc_v[own:].astype(jnp.bfloat16)
    go.store(halo_v, halo_out)
    own_part = mm_nt(delta, ws_v[...])
    base_v[...] = own_part + own_rows(acc_v, own)
    go.store(base_v, base_out)


def last_kernel(
    layer, cols, hid, arr, val, ws, wn, cot, agg_out, delta_out, halo_out, base_out,
    ext_v, val_v, ws_v, wn_v, cot_v, agg_v, delta_v, halo_v, base_v, acc_v, sems,
):
    go = Copies(sems)
    loads = forward_loads(go, layer, hid, arr, val, ws, wn, ext_v, val_v, ws_v, wn_v)
    cot_load = go.start(cot, cot_v)
    pre = pre_activation(loads, cols, hid.shape[0], ext_v, val_v, ws_v, wn_v, agg_v)
    go.store(agg_v, agg_out)
    sigma = jax.nn.sigmoid(pre)
    slope = sigma * (1.0 + pre * (1.0 - sigma))
    cot_load.wait()
    delta = (cot_v[...].astype(jnp.float32) * slope).astype(jnp.bfloat16)
    delta_v[...] = delta
    go.store(delta_v, delta_out)
    spread_back(go, delta, cols, val_v, ws_v, None, wn_v, halo_out, base_out, halo_v, base_v, acc_v)
    go.finish()


def backward_kernel(
    layer, cols, arr, before, slope, row, val, ws, wn, delta_out, halo_out, base_out,
    arr_v, before_v, slope_v, row_v, val_v, ws_v, wn_v, delta_v, halo_v, base_v, acc_v, sems,
):
    go = Copies(sems)
    loads = [
        go.start(row, row_v),
        go.start(arr, arr_v),
        go.start(before, before_v),
        go.start(slope, slope_v),
    ]
    wn_load = go.start(wn.at[layer], wn_v)
    late = [go.start(val, val_v), go.start(ws.at[layer], ws_v)]
    for load in loads[:2]:
        load.wait()
    back = return_rows(row_v[...], arr_v[...], before.shape[0])
    for load in loads[2:]:
        load.wait()
    grad = (before_v[...] + back).astype(jnp.bfloat16)
    delta = (grad.astype(jnp.float32) * slope_v[...]).astype(jnp.bfloat16)
    delta_v[...] = delta
    go.store(delta_v, delta_out)
    for load in late:
        load.wait()
    spread_back(go, delta, cols, val_v, ws_v, wn_load, wn_v, halo_out, base_out, halo_v, base_v, acc_v)
    go.finish()


def final_kernel(arr, before, row, grad_out, arr_v, before_v, row_v, grad_v, sems):
    go = Copies(sems)
    loads = [go.start(row, row_v), go.start(arr, arr_v), go.start(before, before_v)]
    for load in loads:
        load.wait()
    back = return_rows(row_v[...], arr_v[...], before.shape[0])
    grad_v[...] = (before_v[...] + back).astype(jnp.bfloat16)
    go.store(grad_v, grad_out)
    go.finish()


def weight_kernel(core, hid, agg, delta, keep_out, give_out, hid_v, agg_v, delta_v, keep_v, give_v, sems):
    go = Copies(sems)
    mine, other = core[0], 1 - core[0]
    both = (hid_v, agg_v)
    loads = [go.start(delta, delta_v), go.start(hid, hid_v), go.start(agg, agg_v)]
    for load in loads:
        load.wait()
    delta_now = delta_v[...]

    def product(side, target):
        for n, source in enumerate(both):

            @pl.when(side == n)
            def _(source=source):
                target[...] = mm_tn(source[...], delta_now).astype(jnp.bfloat16)

    product(other, give_v)
    go.store(give_v, give_out)
    product(mine, keep_v)
    go.store(keep_v, keep_out)
    go.finish()


def place_kernel(layer, blocks, where, mine, other, *rest):
    self_out, neigh_out, mine_v, other_v, sems = rest[-5:]
    go = Copies(sems)
    loads = [go.start(mine, mine_v), go.start(other, other_v)]
    size = mine.shape[0] // blocks
    for load in loads:
        load.wait()

    def store(source, target, start, first):
        copies = []
        for j in range(blocks):
            to = pl.multiple_of((start ^ j) * size, size)
            copies.append(
                pltpu.make_async_copy(
                    source.at[pl.ds(j * size, size)],
                    target.at[layer, pl.ds(to, size)],
                    sems.at[first + j],
                )
            )
        for copy in copies:
            copy.start()
        for copy in copies:
            copy.wait()

    for core in range(2):

        @pl.when(where[0] == core)
        def _(core=core):
            outs = (self_out, neigh_out)
            store(mine_v, outs[core], where[1], 2)
            store(other_v, outs[1 - core], where[2], 2 + blocks)


def per_device(
    features, cotangent, self_weight, neigh_weight, block_val, block_col, send_idx, send_count
):
    outer = lax.axis_size("gx")
    inner = lax.axis_size("gy")
    devices = outer * inner
    nodes, width = features.shape
    tile = block_val.shape[2]
    layers = self_weight.shape[0]
    slots = send_idx.shape[2]
    halo = devices * slots
    own, far = nodes // tile, halo // tile
    scale = 1.0 / math.sqrt(nodes * devices)
    bf16, f32, i32 = jnp.bfloat16, jnp.float32, jnp.int32

    def call(body, args, outs, scratch, flops=0, alias=None, sems=0, loose=()):
        moved = sum(math.prod(o.shape) * o.dtype.itemsize for o in (*outs, *args))
        count = len(args) + len(outs) + sems
        return pl.pallas_call(
            body,
            in_specs=[
                SMEM if a.ndim == 1 or a is block_col else ANY if n in loose else HBM
                for n, a in enumerate(args)
            ],
            out_specs=[HBM for _ in outs],
            out_shape=[jax.ShapeDtypeStruct(o.shape, o.dtype) for o in outs],
            scratch_shapes=[*scratch, pltpu.SemaphoreType.DMA((count,))],
            input_output_aliases=alias or {},
            cost_estimate=pl.CostEstimate(
                flops=flops, bytes_accessed=moved, transcendentals=0
            ),
            compiler_params=pltpu.CompilerParams(vmem_limit_bytes=62 << 20),
        )(*args)

    rows = pltpu.VMEM((nodes, width), bf16)
    rows32 = pltpu.VMEM((nodes, width), f32)
    tiles = pltpu.VMEM((own, tile, width), bf16)
    halo_tiles = pltpu.VMEM((far, tile, width), bf16)
    halo_rows = pltpu.VMEM((halo, width), bf16)
    ext = pltpu.VMEM((own + far, tile, width), bf16)
    acc = pltpu.VMEM((own + far, tile, width), f32)
    blocks = pltpu.VMEM(block_val.shape, bf16)
    matrix = pltpu.VMEM((width, width), bf16)
    row_list = pltpu.VMEM((1, halo), i32)
    col_list = pltpu.VMEM((halo, 1), i32)
    big = 8 * nodes * width * width

    def exchange(array):
        sent = array.reshape(devices, slots, width)
        return lax.all_to_all(sent, AXES, 0, 0, tiled=True)

    position = lax.axis_index("gy")
    core = position & 1
    core_arg = core.reshape(1)

    bits = list(range(1, inner.bit_length() - 1))
    turn = bits[len(bits) // 2 :] + bits[: len(bits) // 2]
    gx_bits = list(range(outer.bit_length() - 1))
    pieces = 1 << len(bits)

    def flip(array, even, odd):
        perm = [(j, j ^ (1 << (odd if j & 1 else even))) for j in range(inner)]
        return lax.ppermute(array, "gy", perm)

    def bit_of(even, odd):
        return jnp.where(core == 0, (position >> even) & 1, (position >> odd) & 1)

    def reach(order):
        index = jnp.int32(0)
        for bit in order:
            index = index * 2 + ((position >> bit) & 1)
        return index

    mine_at = jnp.where(core == 0, reach(bits), reach(turn))
    other_at = jnp.where(core == 0, reach(turn), reach(bits))
    where = jnp.stack([core, mine_at, other_at]).astype(i32)

    def reduce_all(keep, give):
        parts = [[keep, 0], [flip(give, 0, 0), 0]]
        size = keep.shape[0]

        def rows_at(extra, count):
            total = None
            for array, at in parts:
                piece = lax.dynamic_slice(array, (at + extra, 0), (count, width)).astype(f32)
                total = piece if total is None else total + piece
            return total

        for even, odd in zip(bits, turn):
            size //= 2
            b = bit_of(even, odd)
            theirs = rows_at((1 - b) * size, size).astype(bf16)
            got = flip(theirs, even, odd)
            for part in parts:
                part[1] = part[1] + b * size
            parts.append([got, 0])
        total = rows_at(0, size)
        for bit in gx_bits:
            mine = total.astype(bf16)
            perm = [(j, j ^ (1 << bit)) for j in range(outer)]
            total = mine.astype(f32) + lax.ppermute(mine, "gx", perm).astype(f32)
        piece = (total * scale).astype(bf16)
        for even, odd in zip(bits[::-1], turn[::-1]):
            piece = jnp.concatenate([piece, flip(piece, even, odd)])
        return piece, flip(piece, 0, 0)

    row, col, send = call(
        first_kernel,
        (send_idx, send_count, features),
        (
            jax.ShapeDtypeStruct((1, halo), i32),
            jax.ShapeDtypeStruct((halo, 1), i32),
            jax.ShapeDtypeStruct((halo, width), bf16),
        ),
        (
            pltpu.VMEM(send_idx.shape, i32),
            pltpu.VMEM(send_count.shape, i32),
            rows, row_list, col_list, halo_rows,
        ),
    )
    hidden = features
    hiddens, aggregates, slopes = [features], [], []
    for layer in range(layers - 1):
        arrived = exchange(send)
        aggregate, slope, hidden, send = call(
            functools.partial(middle_kernel, layer),
            (
                block_col, hidden.reshape(own, tile, width), arrived.reshape(far, tile, width),
                block_val, self_weight, neigh_weight, col,
            ),
            (rows, rows32, rows, halo_rows),
            (ext, blocks, matrix, matrix, col_list, rows, rows32, rows, halo_rows),
            big,
            loose=(2,),
        )
        hiddens.append(hidden)
        aggregates.append(aggregate)
        slopes.append(slope)
    arrived = exchange(send)
    aggregate, delta, outgoing, base = call(
        functools.partial(last_kernel, layers - 1),
        (
            block_col, hidden.reshape(own, tile, width), arrived.reshape(far, tile, width),
            block_val, self_weight, neigh_weight, cotangent,
        ),
        (rows, rows, halo_tiles, rows32),
        (ext, blocks, matrix, matrix, rows, rows, rows, halo_tiles, rows32, acc),
        2 * big,
        loose=(2,),
    )
    aggregates.append(aggregate)
    outs = ()
    for layer in reversed(range(layers)):
        arrived = exchange(outgoing).reshape(halo, width)
        keep, give = call(
            weight_kernel,
            (core_arg, hiddens[layer], aggregates[layer], delta),
            (matrix, matrix),
            (rows, rows, rows, matrix, matrix),
            4 * nodes * width * width,
        )
        mine, other = reduce_all(keep, give)
        stacked = jax.ShapeDtypeStruct(self_weight.shape, bf16)
        outs = call(
            functools.partial(place_kernel, layer, pieces),
            (where, mine, other, *outs),
            (stacked, stacked),
            (matrix, matrix),
            alias={3: 0, 4: 1} if outs else None,
            sems=2 * pieces,
            loose=(1, 2),
        )
        if layer:
            delta, outgoing, base = call(
                functools.partial(backward_kernel, layer - 1),
                (
                    block_col, arrived, base, slopes[layer - 1], row,
                    block_val, self_weight, neigh_weight,
                ),
                (rows, halo_tiles, rows32),
                (
                    halo_rows, rows32, rows32, row_list, blocks, matrix, matrix,
                    rows, halo_tiles, rows32, acc,
                ),
                big,
                loose=(1,),
            )
    (grad,) = call(
        final_kernel, (arrived, base, row), (rows,), (halo_rows, rows32, row_list, rows), loose=(0,)
    )
    return (*outs, grad)


def solution(mesh):
    return jax.shard_map(
        per_device,
        mesh=mesh,
        in_specs=(
            P(AXES, None),
            P(AXES, None),
            P(),
            P(),
            P(AXES, None, None, None),
            P(AXES, None),
            P(AXES, None, None),
            P(AXES, None),
        ),
        out_specs=(P(), P(), P(AXES, None)),
        check_vma=False,
    )
```

```python
import functools
import math

import jax
import jax.numpy as jnp
from jax import lax
from jax.experimental import pallas as pl
from jax.experimental.pallas import tpu as pltpu
from jax.sharding import PartitionSpec as P


AXES = ("gx", "gy")


def mm(a, b):
    return jnp.dot(a, b, preferred_element_type=jnp.float32)


def mm_tn(a, b):
    return lax.dot_general(a, b, (((0,), (0,)), ((), ())), preferred_element_type=jnp.float32)


def mm_nt(a, b):
    return lax.dot_general(a, b, (((1,), (1,)), ((), ())), preferred_element_type=jnp.float32)


def iota(shape, dim):
    return lax.broadcasted_iota(jnp.int32, shape, dim)


def ones_where(mask):
    return jnp.where(mask, 1.0, 0.0).astype(jnp.bfloat16)


def pick_rows(col, table):
    hot = ones_where(iota((col.shape[0], table.shape[0]), 1) == col)
    return mm(hot, table).astype(jnp.bfloat16)


def return_rows(row, arrived, nodes):
    hot = ones_where(iota((nodes, row.shape[1]), 0) == row)
    return mm(hot, arrived)


class Copies:
    def __init__(self, sems):
        self.sems, self.used, self.stores = sems, 0, []

    def start(self, source, target):
        copy = pltpu.make_async_copy(source, target, self.sems.at[self.used])
        self.used += 1
        copy.start()
        return copy

    def store(self, source, target):
        self.stores.append(self.start(source, target))

    def finish(self):
        for copy in self.stores:
            copy.wait()


def first_kernel(idx, cnt, table, row_out, col_out, send_out, idx_v, cnt_v, table_v, send_v, sems):
    go = Copies(sems)
    loads = [go.start(idx, idx_v), go.start(cnt, cnt_v), go.start(table, table_v)]
    _, slots, peers = idx.shape
    total = peers * slots
    start_t = iota((total, peers), 1) * slots
    place_t = iota((total, peers), 0)
    inside_t = ones_where((place_t >= start_t) & (place_t < start_t + slots))
    here_t = (iota((total, slots), 0) & (slots - 1)) == iota((total, slots), 1)
    loads[0].wait()
    loads[1].wait()
    live = iota((slots, peers), 0) < jnp.broadcast_to(cnt_v[...], (slots, peers))
    code = jnp.where(live, idx_v[0] + 1, 0).astype(jnp.float32).astype(jnp.bfloat16)
    col = jnp.sum(jnp.where(here_t, mm_nt(inside_t, code), 0.0), axis=1, keepdims=True) - 1.0
    col = col.astype(jnp.int32)
    col_out[...] = col
    loads[2].wait()
    send_v[...] = pick_rows(col, table_v[...])
    go.store(send_v, send_out)
    start = iota((peers, total), 0) * slots
    place = iota((peers, total), 1)
    inside = ones_where((place >= start) & (place < start + slots))
    here = (iota((slots, total), 1) & (slots - 1)) == iota((slots, total), 0)
    row = jnp.sum(jnp.where(here, mm(code, inside), 0.0), axis=0, keepdims=True) - 1.0
    row_out[...] = row.astype(jnp.int32)
    go.finish()


def load_kernel(layer, *refs):
    count = (len(refs) - 1) // 2
    go = Copies(refs[-1])
    for n, (source, target) in enumerate(zip(refs[:count], refs[count:-1])):
        go.store(source.at[layer] if n < 2 else source, target)
    go.finish()


def pre_activation(cols, hid, arr, val, ws, wn, agg_v, ext_v):
    tiles, blocks, tile, _ = val.shape
    own = hid.shape[0] // tile
    for t in range(own):
        ext_v[t] = hid[t * tile : (t + 1) * tile, :]
    for t in range(arr.shape[0] // tile):
        ext_v[own + t] = arr[t * tile : (t + 1) * tile, :]
    for r in range(tiles):
        total = mm(val[r, 0], ext_v[cols[r, 0]])
        for b in range(1, blocks):
            total += mm(val[r, b], ext_v[cols[r, b]])
        agg_v[r * tile : (r + 1) * tile, :] = total.astype(jnp.bfloat16)
    return mm(hid[...], ws[...]) + mm(agg_v[...], wn[...])


def middle_kernel(
    cols, hid, arr, val, ws, wn, col, agg_out, slope_out, next_out, next_near, send_out,
    ext_v, agg_v, slope_v, send_v, sems,
):
    go = Copies(sems)
    pre = pre_activation(cols, hid, arr, val, ws, wn, agg_v, ext_v)
    go.store(agg_v, agg_out)
    sigma = jax.nn.sigmoid(pre)
    hidden = (pre * sigma).astype(jnp.bfloat16)
    next_near[...] = hidden
    go.store(next_near, next_out)
    slope_v[...] = sigma * (1.0 + pre * (1.0 - sigma))
    go.store(slope_v, slope_out)
    send_v[...] = pick_rows(col[...], hidden)
    go.store(send_v, send_out)
    go.finish()


def spread_back(go, delta, cols, val, ws, wn, halo_out, base_out, halo_v, base_v, acc_v):
    tiles, blocks, tile, _ = val.shape
    own = base_out.shape[0] // tile
    acc_v[...] = jnp.zeros_like(acc_v)
    upstream = mm_nt(delta, wn[...]).astype(jnp.bfloat16)
    for r in range(tiles):
        part = upstream[r * tile : (r + 1) * tile, :]
        for b in range(blocks):
            acc_v[cols[r, b]] += mm_tn(val[r, b], part)
    for t in range(halo_out.shape[0] // tile):
        halo_v[t * tile : (t + 1) * tile, :] = acc_v[own + t].astype(jnp.bfloat16)
    go.store(halo_v, halo_out)
    own_part = mm_nt(delta, ws[...])
    for t in range(own):
        at = slice(t * tile, (t + 1) * tile)
        base_v[at, :] = own_part[at, :] + acc_v[t]
    go.store(base_v, base_out)


def last_kernel(
    cols, hid, arr, val, ws, wn, cot, agg_out, delta_out, halo_out, base_out,
    ext_v, agg_v, delta_v, halo_v, base_v, acc_v, sems,
):
    go = Copies(sems)
    pre = pre_activation(cols, hid, arr, val, ws, wn, agg_v, ext_v)
    go.store(agg_v, agg_out)
    sigma = jax.nn.sigmoid(pre)
    slope = sigma * (1.0 + pre * (1.0 - sigma))
    delta = (cot[...].astype(jnp.float32) * slope).astype(jnp.bfloat16)
    delta_v[...] = delta
    go.store(delta_v, delta_out)
    spread_back(go, delta, cols, val, ws, wn, halo_out, base_out, halo_v, base_v, acc_v)
    go.finish()


def delta_of(loads, arr, row, before_v, slope_v):
    back = return_rows(row[...], arr[...], before_v.shape[0])
    for load in loads:
        load.wait()
    grad = (before_v[...] + back).astype(jnp.bfloat16)
    return (grad.astype(jnp.float32) * slope_v[...]).astype(jnp.bfloat16)


def backward_kernel(
    cols, arr, before, slope, row, val, ws, wn, delta_out, halo_out, base_out,
    before_v, slope_v, delta_v, halo_v, base_v, acc_v, sems,
):
    go = Copies(sems)
    loads = [go.start(before, before_v), go.start(slope, slope_v)]
    delta = delta_of(loads, arr, row, before_v, slope_v)
    delta_v[...] = delta
    go.store(delta_v, delta_out)
    spread_back(go, delta, cols, val, ws, wn, halo_out, base_out, halo_v, base_v, acc_v)
    go.finish()


def spread_kernel(cols, delta, val, ws, wn, halo_out, base_out, halo_v, base_v, acc_v, sems):
    go = Copies(sems)
    spread_back(go, delta[...], cols, val, ws, wn, halo_out, base_out, halo_v, base_v, acc_v)
    go.finish()


def final_kernel(arr, before, row, grad_out, before_v, grad_v, sems):
    go = Copies(sems)
    load = go.start(before, before_v)
    back = return_rows(row[...], arr[...], before.shape[0])
    load.wait()
    grad_v[...] = (before_v[...] + back).astype(jnp.bfloat16)
    go.store(grad_v, grad_out)
    go.finish()


def products(core, hid_v, agg_v, delta, pairs):
    for side, target in ((1 - core, pairs[0]), (core, pairs[1])):
        for n, source in enumerate((hid_v, agg_v)):

            @pl.when(side == n)
            def _(source=source, target=target):
                target[...] = mm_tn(source[...], delta).astype(jnp.bfloat16)


def weight_kernel(core, hid, agg, delta, keep_out, give, hid_v, agg_v, delta_v, keep_v, sems):
    go = Copies(sems)
    loads = [go.start(delta, delta_v), go.start(hid, hid_v), go.start(agg, agg_v)]
    for load in loads:
        load.wait()
    products(core[0], hid_v, agg_v, delta_v[...], (give, keep_v))
    go.store(keep_v, keep_out)
    go.finish()


def top_kernel(
    core, hid, agg, arr, before, slope, row, delta_near, keep_out, give,
    before_v, slope_v, hid_v, agg_v, keep_v, sems,
):
    go = Copies(sems)
    loads = [go.start(before, before_v), go.start(slope, slope_v)]
    late = [go.start(hid, hid_v), go.start(agg, agg_v)]
    delta = delta_of(loads, arr, row, before_v, slope_v)
    delta_near[...] = delta
    for load in late:
        load.wait()
    products(core[0], hid_v, agg_v, delta, (give, keep_v))
    go.store(keep_v, keep_out)
    go.finish()


def quarters_kernel(chip, keep, got, *rest):
    count = len(rest) - 4
    outs, (keep_v, got_v, out_v, sems) = rest[:count], rest[count:]
    go = Copies(sems)
    size = keep.shape[0] // count
    loads = []
    for m in range(count):
        at = pl.multiple_of((chip[0] ^ m) * size, size)
        here = pl.ds(m * size, size)
        loads.append(go.start(keep.at[pl.ds(at, size)], keep_v.at[here]))
        loads.append(go.start(got.at[pl.ds(at, size)], got_v.at[here]))
    for m in range(count):
        loads[2 * m].wait()
        loads[2 * m + 1].wait()
        here = pl.ds(m * size, size)
        total = keep_v[here, :].astype(jnp.float32) + got_v[here, :].astype(jnp.float32)
        out_v[here, :] = total.astype(jnp.bfloat16)
        go.store(out_v.at[here], outs[m])
    go.finish()


def place_kernel(layers, count, where, *refs):
    mine, other = refs[:count], refs[count : 2 * count]
    self_out, neigh_out, sems = refs[-3:]
    size = mine[0].shape[0] // len(layers)
    for core, outs in enumerate(((self_out, neigh_out), (neigh_out, self_out))):

        @pl.when(where[0] == core)
        def _(outs=outs):
            copies = []
            for m, source in enumerate((*mine, *other)):
                to = pl.multiple_of((where[1] ^ (m % count)) * size, size)
                for n, layer in enumerate(layers):
                    copies.append(
                        pltpu.make_async_copy(
                            source.at[pl.ds(n * size, size)],
                            outs[m // count].at[layer, pl.ds(to, size)],
                            sems.at[len(copies)],
                        )
                    )
            for copy in copies:
                copy.start()
            for copy in copies:
                copy.wait()


def per_device(
    features, cotangent, self_weight, neigh_weight, block_val, block_col, send_idx, send_count
):
    outer = lax.axis_size("gx")
    inner = lax.axis_size("gy")
    devices = outer * inner
    nodes, width = features.shape
    tile = block_val.shape[2]
    layers = self_weight.shape[0]
    slots = send_idx.shape[2]
    halo = devices * slots
    ext_tiles = (nodes + halo) // tile
    scale = 1.0 / math.sqrt(nodes * devices)
    bf16, f32, i32 = jnp.bfloat16, jnp.float32, jnp.int32
    near, away, scalars = pltpu.VMEM, pltpu.HBM, pltpu.SMEM

    def call(body, args, outs, scratch=(), sems=None, flops=0, alias=None):
        moved = sum(math.prod(o[0]) * jnp.dtype(o[1]).itemsize for o in outs)
        operands = [
            a if space is scalars else pltpu.with_memory_space_constraint(a, space)
            for a, space in args
        ]
        sems = len(args) + len(outs) if sems is None else sems
        return pl.pallas_call(
            body,
            in_specs=[pl.BlockSpec(memory_space=space) for _, space in args],
            out_specs=[pl.BlockSpec(memory_space=o[2]) for o in outs],
            out_shape=[o[2](o[0], o[1]) for o in outs],
            scratch_shapes=[*(pltpu.VMEM(*s) for s in scratch), pltpu.SemaphoreType.DMA((sems,))],
            input_output_aliases=alias or {},
            cost_estimate=pl.CostEstimate(
                flops=flops, bytes_accessed=2 * moved, transcendentals=0
            ),
            compiler_params=pltpu.CompilerParams(vmem_limit_bytes=16 << 20),
        )(*operands)

    rows, rows32 = ((nodes, width), bf16), ((nodes, width), f32)
    square, halo_rows = ((width, width), bf16), ((halo, width), bf16)
    ext, acc = ((ext_tiles, tile, width), bf16), ((ext_tiles, tile, width), f32)
    big = 8 * nodes * width * width

    def exchange(array):
        sent = array.reshape(devices, slots, width)
        return lax.all_to_all(sent, AXES, 0, 0, tiled=True).reshape(halo, width)

    position = lax.axis_index("gy")
    core, chip = position & 1, position >> 1
    core_arg = core.reshape(1)
    chips = inner // 2
    gx_bits = list(range(outer.bit_length() - 1))

    def flip(array, mask):
        return lax.ppermute(array, "gy", [(j, j ^ mask) for j in range(inner)])

    def chip_sum(keep, give):
        got = flip(give, 1)
        mine, *others = call(
            quarters_kernel,
            ((chip.reshape(1), scalars), (keep, away), (got, near)),
            (((width // chips, width), bf16, near),) * chips,
            (square, square, square),
            3 * chips,
        )
        total = mine.astype(f32)
        for m, other in enumerate(others, 1):
            arrival = flip(other, 2 * m)
            total = total + arrival.astype(f32)
        for bit in gx_bits:
            mine = total.astype(bf16)
            perm = [(j, j ^ (1 << bit)) for j in range(outer)]
            total = mine.astype(f32) + lax.ppermute(mine, "gx", perm).astype(f32)
        return (total * scale).astype(bf16)

    def gather(piece):
        mine, other = [piece], []
        for m in range(1, chips):
            mine.append(flip(piece, 2 * m))
        for m in range(chips):
            other.append(flip(mine[m], 1))
        return mine, other

    where = jnp.stack([core, chip]).astype(i32)

    def place(group, mine, other, outs):
        return call(
            functools.partial(place_kernel, group, chips),
            ((where, scalars), *((a, near) for a in (*mine, *other)), *((o, away) for o in outs)),
            ((self_weight.shape, bf16, away),) * 2,
            (),
            2 * chips * len(group),
            alias={1 + 2 * chips: 0, 2 + 2 * chips: 1} if outs else None,
        )

    def load(layer, *others):
        arrays = (self_weight, neigh_weight, *others)
        return call(
            functools.partial(load_kernel, layer),
            [(a, away) for a in arrays],
            [(a.shape[1:] if n < 2 else a.shape, a.dtype, near) for n, a in enumerate(arrays)],
        )

    cols = (block_col, scalars)
    row, col, send = call(
        first_kernel,
        ((send_idx.transpose(0, 2, 1), away), (send_count, away), (features, away)),
        (((1, halo), i32, near), ((halo, 1), i32, near), (*halo_rows, away)),
        (
            ((1, slots, devices), i32), ((1, devices), i32), rows, halo_rows,
        ),
    )
    arrived = exchange(send)
    ws, wn, hidden, val = load(0, features, block_val)
    hiddens, aggregates, slopes = [features], [], []
    for layer in range(layers - 1):
        aggregate, slope, kept, hidden, send = call(
            middle_kernel,
            (
                cols, (hidden, near), (arrived, near), (val, near), (ws, near), (wn, near),
                (col, near),
            ),
            ((*rows, away), (*rows32, away), (*rows, away), (*rows, near), (*halo_rows, away)),
            (ext, rows, rows32, halo_rows),
            flops=big,
        )
        hiddens.append(kept)
        aggregates.append(aggregate)
        slopes.append(slope)
        arrived = exchange(send)
        last = layer + 2 == layers
        ws, wn, *cot = load(layer + 1, *((cotangent,) if last else ()))
    aggregate, delta, outgoing, base = call(
        last_kernel,
        (
            cols, (hidden, near), (arrived, near), (val, near), (ws, near), (wn, near),
            (cot[0], near),
        ),
        ((*rows, away), (*rows, away), (*halo_rows, away), (*rows32, away)),
        (ext, rows, rows, halo_rows, rows32, acc),
        flops=2 * big,
    )
    aggregates.append(aggregate)
    sums = []
    for layer in reversed(range(layers)):
        below = layer - 1
        if layer:
            keep, give = call(
                weight_kernel,
                (
                    (core_arg, scalars), (hiddens[layer], away), (aggregates[layer], away),
                    (delta, away),
                ),
                ((*square, away), (*square, near)),
                (rows, rows, rows, square),
                flops=big // 2,
            )
        sums.append(chip_sum(keep, give))
        arrived = exchange(outgoing)
        if layer:
            ws, wn = load(below)
        if below > 0:
            delta, outgoing, base = call(
                backward_kernel,
                (
                    cols, (arrived, near), (base, away), (slopes[below], away), (row, near),
                    (val, near), (ws, near), (wn, near),
                ),
                ((*rows, away), (*halo_rows, away), (*rows32, away)),
                (rows32, rows32, rows, halo_rows, rows32, acc),
                flops=big,
            )
        elif below == 0:
            delta, keep, give = call(
                top_kernel,
                (
                    (core_arg, scalars), (hiddens[0], away), (aggregates[0], away),
                    (arrived, near), (base, away), (slopes[0], away), (row, near),
                ),
                ((*rows, near), (*square, away), (*square, near)),
                (rows32, rows32, rows, rows, square),
                flops=big,
            )
            outgoing, base = call(
                spread_kernel,
                (cols, (delta, near), (val, near), (ws, near), (wn, near)),
                ((*halo_rows, away), (*rows32, away)),
                (halo_rows, rows32, acc),
                flops=big,
            )
    (grad,) = call(
        final_kernel, ((arrived, near), (base, away), (row, near)), ((*rows, away),), (rows32, rows)
    )
    mine, other = gather(jnp.concatenate(sums[:-1]))
    outs = place(tuple(reversed(range(1, layers))), mine, other, ())
    mine, other = gather(sums[-1])
    outs = place((0,), mine, other, outs)
    return (*outs, grad)


def solution(mesh):
    return jax.shard_map(
        per_device,
        mesh=mesh,
        in_specs=(
            P(AXES, None),
            P(AXES, None),
            P(),
            P(),
            P(AXES, None, None, None),
            P(AXES, None),
            P(AXES, None, None),
            P(AXES, None),
        ),
        out_specs=(P(), P(), P(AXES, None)),
        check_vma=False,
    )
```

```python
import functools
import math

import jax
import jax.numpy as jnp
from jax import lax
from jax.experimental import pallas as pl
from jax.experimental.pallas import tpu as pltpu
from jax.sharding import PartitionSpec as P


AXES = ("gx", "gy")


def mm(a, b):
    return jnp.dot(a, b, preferred_element_type=jnp.float32)


def mm_tn(a, b):
    return lax.dot_general(a, b, (((0,), (0,)), ((), ())), preferred_element_type=jnp.float32)


def mm_nt(a, b):
    return lax.dot_general(a, b, (((1,), (1,)), ((), ())), preferred_element_type=jnp.float32)


def iota(shape, dim):
    return lax.broadcasted_iota(jnp.int32, shape, dim)


def ones_where(mask):
    return jnp.where(mask, 1.0, 0.0).astype(jnp.bfloat16)


def pick_rows(col, table):
    hot = ones_where(iota((col.shape[0], table.shape[0]), 1) == col)
    return mm(hot, table).astype(jnp.bfloat16)


def return_rows(row, arrived, nodes):
    hot = ones_where(iota((nodes, row.shape[1]), 0) == row)
    return mm(hot, arrived)


class Copies:
    def __init__(self, sems):
        self.sems, self.used, self.stores = sems, 0, []

    def start(self, source, target):
        copy = pltpu.make_async_copy(source, target, self.sems.at[self.used])
        self.used += 1
        copy.start()
        return copy

    def store(self, source, target):
        self.stores.append(self.start(source, target))

    def finish(self):
        for copy in self.stores:
            copy.wait()


def first_kernel(idx, cnt, table, row_out, col_out, send_out, idx_v, cnt_v, table_v, send_v, sems):
    go = Copies(sems)
    loads = [go.start(idx, idx_v), go.start(cnt, cnt_v), go.start(table, table_v)]
    _, slots, peers = idx.shape
    total = peers * slots
    start_t = iota((total, peers), 1) * slots
    place_t = iota((total, peers), 0)
    inside_t = ones_where((place_t >= start_t) & (place_t < start_t + slots))
    here_t = (iota((total, slots), 0) & (slots - 1)) == iota((total, slots), 1)
    loads[0].wait()
    loads[1].wait()
    live = iota((slots, peers), 0) < jnp.broadcast_to(cnt_v[...], (slots, peers))
    code = jnp.where(live, idx_v[0] + 1, 0).astype(jnp.float32).astype(jnp.bfloat16)
    col = jnp.sum(jnp.where(here_t, mm_nt(inside_t, code), 0.0), axis=1, keepdims=True) - 1.0
    col = col.astype(jnp.int32)
    col_out[...] = col
    loads[2].wait()
    send_v[...] = pick_rows(col, table_v[...])
    go.store(send_v, send_out)
    start = iota((peers, total), 0) * slots
    place = iota((peers, total), 1)
    inside = ones_where((place >= start) & (place < start + slots))
    here = (iota((slots, total), 1) & (slots - 1)) == iota((slots, total), 0)
    row = jnp.sum(jnp.where(here, mm(code, inside), 0.0), axis=0, keepdims=True) - 1.0
    row_out[...] = row.astype(jnp.int32)
    go.finish()


def load_kernel(layer, *refs):
    count = (len(refs) - 1) // 2
    go = Copies(refs[-1])
    for n, (source, target) in enumerate(zip(refs[:count], refs[count:-1])):
        go.store(source.at[layer] if n < 2 else source, target)
    go.finish()


def pre_activation(cols, hid, arr, val, ws, wn, agg_v, ext_v):
    tiles, blocks, tile, _ = val.shape
    own = hid.shape[0] // tile
    for t in range(own):
        ext_v[t] = hid[t * tile : (t + 1) * tile, :]
    for t in range(arr.shape[0] // tile):
        ext_v[own + t] = arr[t * tile : (t + 1) * tile, :]
    for r in range(tiles):
        total = mm(val[r, 0], ext_v[cols[r, 0]])
        for b in range(1, blocks):
            total += mm(val[r, b], ext_v[cols[r, b]])
        agg_v[r * tile : (r + 1) * tile, :] = total.astype(jnp.bfloat16)
    return mm(hid[...], ws[...]) + mm(agg_v[...], wn[...])


def middle_kernel(
    cols, hid, arr, val, ws, wn, col, agg_out, slope_out, next_out, next_near, send_out,
    ext_v, agg_v, slope_v, send_v, sems,
):
    go = Copies(sems)
    pre = pre_activation(cols, hid, arr, val, ws, wn, agg_v, ext_v)
    go.store(agg_v, agg_out)
    sigma = jax.nn.sigmoid(pre)
    hidden = (pre * sigma).astype(jnp.bfloat16)
    next_near[...] = hidden
    go.store(next_near, next_out)
    slope_v[...] = sigma * (1.0 + pre * (1.0 - sigma))
    go.store(slope_v, slope_out)
    send_v[...] = pick_rows(col[...], hidden)
    go.store(send_v, send_out)
    go.finish()


def spread_back(go, delta, cols, val, ws, wn, halo_out, base_out, halo_v, base_v, acc_v):
    tiles, blocks, tile, _ = val.shape
    own = base_out.shape[0] // tile
    acc_v[...] = jnp.zeros_like(acc_v)
    upstream = mm_nt(delta, wn[...]).astype(jnp.bfloat16)
    for r in range(tiles):
        part = upstream[r * tile : (r + 1) * tile, :]
        for b in range(blocks):
            acc_v[cols[r, b]] += mm_tn(val[r, b], part)
    for t in range(halo_out.shape[0] // tile):
        halo_v[t * tile : (t + 1) * tile, :] = acc_v[own + t].astype(jnp.bfloat16)
    go.store(halo_v, halo_out)
    own_part = mm_nt(delta, ws[...])
    for t in range(own):
        at = slice(t * tile, (t + 1) * tile)
        base_v[at, :] = own_part[at, :] + acc_v[t]
    go.store(base_v, base_out)


def last_kernel(
    cols, hid, arr, val, ws, wn, cot, agg_out, delta_out, halo_out, base_out,
    ext_v, agg_v, delta_v, halo_v, base_v, acc_v, sems,
):
    go = Copies(sems)
    pre = pre_activation(cols, hid, arr, val, ws, wn, agg_v, ext_v)
    go.store(agg_v, agg_out)
    sigma = jax.nn.sigmoid(pre)
    slope = sigma * (1.0 + pre * (1.0 - sigma))
    delta = (cot[...].astype(jnp.float32) * slope).astype(jnp.bfloat16)
    delta_v[...] = delta
    go.store(delta_v, delta_out)
    spread_back(go, delta, cols, val, ws, wn, halo_out, base_out, halo_v, base_v, acc_v)
    go.finish()


def delta_of(loads, arr, row, before_v, slope_v):
    back = return_rows(row[...], arr[...], before_v.shape[0])
    for load in loads:
        load.wait()
    grad = (before_v[...] + back).astype(jnp.bfloat16)
    return (grad.astype(jnp.float32) * slope_v[...]).astype(jnp.bfloat16)


def backward_kernel(
    cols, arr, before, slope, row, val, ws, wn, delta_out, halo_out, base_out,
    before_v, slope_v, halo_v, base_v, acc_v, sems,
):
    go = Copies(sems)
    loads = [go.start(before, before_v), go.start(slope, slope_v)]
    delta = delta_of(loads, arr, row, before_v, slope_v)
    delta_out[...] = delta
    spread_back(go, delta, cols, val, ws, wn, halo_out, base_out, halo_v, base_v, acc_v)
    go.finish()


def final_kernel(arr, before, row, grad_out, before_v, grad_v, sems):
    go = Copies(sems)
    load = go.start(before, before_v)
    back = return_rows(row[...], arr[...], before.shape[0])
    load.wait()
    grad_v[...] = (before_v[...] + back).astype(jnp.bfloat16)
    go.store(grad_v, grad_out)
    go.finish()


def products(core, hid_v, agg_v, delta, pairs):
    for side, target in ((1 - core, pairs[0]), (core, pairs[1])):
        for n, source in enumerate((hid_v, agg_v)):

            @pl.when(side == n)
            def _(source=source, target=target):
                target[...] = mm_tn(source[...], delta).astype(jnp.bfloat16)


def weight_kernel(core, hid, agg, delta, keep, give, hid_v, agg_v, delta_v, sems):
    go = Copies(sems)
    loads = [go.start(delta, delta_v), go.start(hid, hid_v), go.start(agg, agg_v)]
    for load in loads:
        load.wait()
    products(core[0], hid_v, agg_v, delta_v[...], (give, keep))


def near_weight_kernel(core, hid, agg, delta, keep, give, sems):
    products(core[0], hid, agg, delta[...], (give, keep))


def quarters_kernel(chip, keep, got, *outs):
    size = outs[0].shape[0]
    for m, out in enumerate(outs[:-1]):
        at = pl.ds(pl.multiple_of((chip[0] ^ m) * size, size), size)
        total = keep[at, :].astype(jnp.float32) + got[at, :].astype(jnp.float32)
        out[...] = total.astype(jnp.bfloat16)


def place_kernel(layers, count, where, *refs):
    mine, other = refs[:count], refs[count : 2 * count]
    self_out, neigh_out, sems = refs[-3:]
    size = mine[0].shape[0] // len(layers)
    for core, outs in enumerate(((self_out, neigh_out), (neigh_out, self_out))):

        @pl.when(where[0] == core)
        def _(outs=outs):
            copies = []
            for m, source in enumerate((*mine, *other)):
                to = pl.multiple_of((where[1] ^ (m % count)) * size, size)
                for n, layer in enumerate(layers):
                    copies.append(
                        pltpu.make_async_copy(
                            source.at[pl.ds(n * size, size)],
                            outs[m // count].at[layer, pl.ds(to, size)],
                            sems.at[len(copies)],
                        )
                    )
            for copy in copies:
                copy.start()
            for copy in copies:
                copy.wait()


def per_device(
    features, cotangent, self_weight, neigh_weight, block_val, block_col, send_idx, send_count
):
    outer = lax.axis_size("gx")
    inner = lax.axis_size("gy")
    devices = outer * inner
    nodes, width = features.shape
    tile = block_val.shape[2]
    layers = self_weight.shape[0]
    slots = send_idx.shape[2]
    halo = devices * slots
    ext_tiles = (nodes + halo) // tile
    scale = 1.0 / math.sqrt(nodes * devices)
    bf16, f32, i32 = jnp.bfloat16, jnp.float32, jnp.int32
    near, away, scalars = pltpu.VMEM, pltpu.HBM, pltpu.SMEM

    def call(body, args, outs, scratch=(), sems=None, flops=0, alias=None):
        moved = sum(math.prod(o[0]) * jnp.dtype(o[1]).itemsize for o in outs)
        operands = [
            a if space is scalars else pltpu.with_memory_space_constraint(a, space)
            for a, space in args
        ]
        sems = len(args) + len(outs) if sems is None else sems
        return pl.pallas_call(
            body,
            in_specs=[pl.BlockSpec(memory_space=space) for _, space in args],
            out_specs=[pl.BlockSpec(memory_space=o[2]) for o in outs],
            out_shape=[o[2](o[0], o[1]) for o in outs],
            scratch_shapes=[*(pltpu.VMEM(*s) for s in scratch), pltpu.SemaphoreType.DMA((sems,))],
            input_output_aliases=alias or {},
            cost_estimate=pl.CostEstimate(
                flops=flops, bytes_accessed=2 * moved, transcendentals=0
            ),
            compiler_params=pltpu.CompilerParams(vmem_limit_bytes=16 << 20),
        )(*operands)

    rows, rows32 = ((nodes, width), bf16), ((nodes, width), f32)
    square, halo_rows = ((width, width), bf16), ((halo, width), bf16)
    ext, acc = ((ext_tiles, tile, width), bf16), ((ext_tiles, tile, width), f32)
    big = 8 * nodes * width * width

    def exchange(array):
        sent = array.reshape(devices, slots, width)
        return lax.all_to_all(sent, AXES, 0, 0, tiled=True).reshape(halo, width)

    position = lax.axis_index("gy")
    core, chip = position & 1, position >> 1
    core_arg = core.reshape(1)
    chips = inner // 2
    gx_bits = list(range(outer.bit_length() - 1))

    def flip(array, mask):
        return lax.ppermute(array, "gy", [(j, j ^ mask) for j in range(inner)])

    def chip_sum(keep, give):
        got = flip(give, 1)
        mine, *others = call(
            quarters_kernel,
            ((chip.reshape(1), scalars), (keep, near), (got, near)),
            (((width // chips, width), bf16, near),) * chips,
        )
        total = mine.astype(f32)
        for m, other in enumerate(others, 1):
            arrival = flip(other, 2 * m)
            total = total + arrival.astype(f32)
        for bit in gx_bits:
            mine = total.astype(bf16)
            perm = [(j, j ^ (1 << bit)) for j in range(outer)]
            total = mine.astype(f32) + lax.ppermute(mine, "gx", perm).astype(f32)
        return (total * scale).astype(bf16)

    def gather(piece):
        mine, other = [piece], []
        for m in range(1, chips):
            mine.append(flip(piece, 2 * m))
        for m in range(chips):
            other.append(flip(mine[m], 1))
        return mine, other

    where = jnp.stack([core, chip]).astype(i32)

    def place(group, mine, other, outs):
        return call(
            functools.partial(place_kernel, group, chips),
            ((where, scalars), *((a, near) for a in (*mine, *other)), *((o, away) for o in outs)),
            ((self_weight.shape, bf16, away),) * 2,
            (),
            2 * chips * len(group),
            alias={1 + 2 * chips: 0, 2 + 2 * chips: 1} if outs else None,
        )

    def load(layer, *others):
        arrays = (self_weight, neigh_weight, *others)
        return call(
            functools.partial(load_kernel, layer),
            [(a, away) for a in arrays],
            [(a.shape[1:] if n < 2 else a.shape, a.dtype, near) for n, a in enumerate(arrays)],
        )

    cols = (block_col, scalars)
    row, col, send = call(
        first_kernel,
        ((send_idx.transpose(0, 2, 1), away), (send_count, away), (features, away)),
        (((1, halo), i32, near), ((halo, 1), i32, near), (*halo_rows, away)),
        (
            ((1, slots, devices), i32), ((1, devices), i32), rows, halo_rows,
        ),
    )
    arrived = exchange(send)
    ws, wn, hidden, val = load(0, features, block_val)
    hiddens, aggregates, slopes = [features], [], []
    for layer in range(layers - 1):
        aggregate, slope, kept, hidden, send = call(
            middle_kernel,
            (
                cols, (hidden, near), (arrived, near), (val, near), (ws, near), (wn, near),
                (col, near),
            ),
            ((*rows, away), (*rows32, away), (*rows, away), (*rows, near), (*halo_rows, away)),
            (ext, rows, rows32, halo_rows),
            flops=big,
        )
        hiddens.append(kept)
        aggregates.append(aggregate)
        slopes.append(slope)
        arrived = exchange(send)
        last = layer + 2 == layers
        ws, wn, *cot = load(layer + 1, *((cotangent,) if last else ()))
    aggregate, delta, outgoing, base = call(
        last_kernel,
        (
            cols, (hidden, near), (arrived, near), (val, near), (ws, near), (wn, near),
            (cot[0], near),
        ),
        ((*rows, away), (*rows, away), (*halo_rows, away), (*rows32, away)),
        (ext, rows, rows, halo_rows, rows32, acc),
        flops=2 * big,
    )
    aggregates.append(aggregate)
    sums, delta_at = [], away
    for layer in reversed(range(layers)):
        below = layer - 1
        if layer:
            sources = ((hiddens[layer], away), (aggregates[layer], away), (delta, delta_at))
        else:
            sources = ((hid, near), (agg, near), (delta, near))
        keep, give = call(
            weight_kernel if layer else near_weight_kernel,
            ((core_arg, scalars), *sources),
            ((*square, near), (*square, near)),
            (rows, rows, rows) if layer else (),
            flops=big // 2,
        )
        sums.append(chip_sum(keep, give))
        arrived = exchange(outgoing)
        if layer:
            last = (hiddens[0], aggregates[0]) if below == 0 else ()
            ws, wn, *more = load(below, *last)
            if more:
                hid, agg = more
            delta_at = near
            delta, outgoing, base = call(
                backward_kernel,
                (
                    cols, (arrived, near), (base, away), (slopes[below], away), (row, near),
                    (val, near), (ws, near), (wn, near),
                ),
                ((*rows, near), (*halo_rows, away), (*rows32, away)),
                (rows32, rows32, halo_rows, rows32, acc),
                flops=big,
            )
    (grad,) = call(
        final_kernel, ((arrived, near), (base, away), (row, near)), ((*rows, away),), (rows32, rows)
    )
    mine, other = gather(jnp.concatenate(sums[:-1]))
    outs = place(tuple(reversed(range(1, layers))), mine, other, ())
    mine, other = gather(sums[-1])
    outs = place((0,), mine, other, outs)
    return (*outs, grad)


def solution(mesh):
    return jax.shard_map(
        per_device,
        mesh=mesh,
        in_specs=(
            P(AXES, None),
            P(AXES, None),
            P(),
            P(),
            P(AXES, None, None, None),
            P(AXES, None),
            P(AXES, None, None),
            P(AXES, None),
        ),
        out_specs=(P(), P(), P(AXES, None)),
        check_vma=False,
    )
```

```python
import functools
import math

import jax
import jax.numpy as jnp
from jax import lax
from jax.experimental import pallas as pl
from jax.experimental.pallas import tpu as pltpu
from jax.sharding import PartitionSpec as P


AXES = ("gx", "gy")


def mm(a, b):
    return jnp.dot(a, b, preferred_element_type=jnp.float32)


def mm_tn(a, b):
    return lax.dot_general(a, b, (((0,), (0,)), ((), ())), preferred_element_type=jnp.float32)


def mm_nt(a, b):
    return lax.dot_general(a, b, (((1,), (1,)), ((), ())), preferred_element_type=jnp.float32)


def iota(shape, dim):
    return lax.broadcasted_iota(jnp.int32, shape, dim)


def ones_where(mask):
    return jnp.where(mask, 1.0, 0.0).astype(jnp.bfloat16)


def pick_rows(col, table):
    hot = ones_where(iota((col.shape[0], table.shape[0]), 1) == col)
    return mm(hot, table).astype(jnp.bfloat16)


def return_rows(row, arrived, nodes):
    hot = ones_where(iota((nodes, row.shape[1]), 0) == row)
    return mm(hot, arrived)


class Copies:
    def __init__(self, sems):
        self.sems, self.used, self.stores = sems, 0, []

    def start(self, source, target):
        copy = pltpu.make_async_copy(source, target, self.sems.at[self.used])
        self.used += 1
        copy.start()
        return copy

    def store(self, source, target):
        self.stores.append(self.start(source, target))

    def finish(self):
        for copy in self.stores:
            copy.wait()


def first_kernel(idx, cnt, table, row_out, col_out, send_out, idx_v, cnt_v, table_v, send_v, sems):
    go = Copies(sems)
    loads = [go.start(idx, idx_v), go.start(cnt, cnt_v), go.start(table, table_v)]
    _, slots, peers = idx.shape
    total = peers * slots
    start_t = iota((total, peers), 1) * slots
    place_t = iota((total, peers), 0)
    inside_t = ones_where((place_t >= start_t) & (place_t < start_t + slots))
    here_t = (iota((total, slots), 0) & (slots - 1)) == iota((total, slots), 1)
    loads[0].wait()
    loads[1].wait()
    live = iota((slots, peers), 0) < jnp.broadcast_to(cnt_v[...], (slots, peers))
    code = jnp.where(live, idx_v[0] + 1, 0).astype(jnp.float32).astype(jnp.bfloat16)
    col = jnp.sum(jnp.where(here_t, mm_nt(inside_t, code), 0.0), axis=1, keepdims=True) - 1.0
    col = col.astype(jnp.int32)
    col_out[...] = col
    loads[2].wait()
    send_v[...] = pick_rows(col, table_v[...])
    go.store(send_v, send_out)
    start = iota((peers, total), 0) * slots
    place = iota((peers, total), 1)
    inside = ones_where((place >= start) & (place < start + slots))
    here = (iota((slots, total), 1) & (slots - 1)) == iota((slots, total), 0)
    row = jnp.sum(jnp.where(here, mm(code, inside), 0.0), axis=0, keepdims=True) - 1.0
    row_out[...] = row.astype(jnp.int32)
    go.finish()


def load_kernel(layer, *refs):
    count = (len(refs) - 1) // 2
    go = Copies(refs[-1])
    for n, (source, target) in enumerate(zip(refs[:count], refs[count:-1])):
        go.store(source.at[layer] if n < 2 else source, target)
    go.finish()


def pre_activation(cols, hid, arr, val, ws, wn, agg_v, ext_v):
    tiles, blocks, tile, _ = val.shape
    own = hid.shape[0] // tile
    for t in range(own):
        ext_v[t] = hid[t * tile : (t + 1) * tile, :]
    for t in range(arr.shape[0] // tile):
        ext_v[own + t] = arr[t * tile : (t + 1) * tile, :]
    for r in range(tiles):
        total = mm(val[r, 0], ext_v[cols[r, 0]])
        for b in range(1, blocks):
            total += mm(val[r, b], ext_v[cols[r, b]])
        agg_v[r * tile : (r + 1) * tile, :] = total.astype(jnp.bfloat16)
    return mm(hid[...], ws[...]) + mm(agg_v[...], wn[...])


def middle_kernel(
    cols, hid, arr, val, ws, wn, col, agg_out, slope_out, next_out, next_near, send_out,
    ext_v, agg_v, slope_v, send_v, sems,
):
    go = Copies(sems)
    pre = pre_activation(cols, hid, arr, val, ws, wn, agg_v, ext_v)
    go.store(agg_v, agg_out)
    sigma = jax.nn.sigmoid(pre)
    hidden = (pre * sigma).astype(jnp.bfloat16)
    next_near[...] = hidden
    go.store(next_near, next_out)
    slope_v[...] = sigma * (1.0 + pre * (1.0 - sigma))
    go.store(slope_v, slope_out)
    send_v[...] = pick_rows(col[...], hidden)
    go.store(send_v, send_out)
    go.finish()


def spread_back(go, delta, cols, val, ws, wn, halo_out, base_out, halo_v, base_v, acc_v):
    tiles, blocks, tile, _ = val.shape
    own = base_out.shape[0] // tile
    acc_v[...] = jnp.zeros_like(acc_v)
    upstream = mm_nt(delta, wn[...]).astype(jnp.bfloat16)
    for r in range(tiles):
        part = upstream[r * tile : (r + 1) * tile, :]
        for b in range(blocks):
            acc_v[cols[r, b]] += mm_tn(val[r, b], part)
    for t in range(halo_out.shape[0] // tile):
        halo_v[t * tile : (t + 1) * tile, :] = acc_v[own + t].astype(jnp.bfloat16)
    go.store(halo_v, halo_out)
    own_part = mm_nt(delta, ws[...])
    for t in range(own):
        at = slice(t * tile, (t + 1) * tile)
        base_v[at, :] = own_part[at, :] + acc_v[t]
    go.store(base_v, base_out)


def last_kernel(
    cols, hid, arr, val, ws, wn, cot, agg_out, delta_out, halo_out, base_out,
    ext_v, agg_v, delta_v, halo_v, base_v, acc_v, sems,
):
    go = Copies(sems)
    pre = pre_activation(cols, hid, arr, val, ws, wn, agg_v, ext_v)
    go.store(agg_v, agg_out)
    sigma = jax.nn.sigmoid(pre)
    slope = sigma * (1.0 + pre * (1.0 - sigma))
    delta = (cot[...].astype(jnp.float32) * slope).astype(jnp.bfloat16)
    delta_v[...] = delta
    go.store(delta_v, delta_out)
    spread_back(go, delta, cols, val, ws, wn, halo_out, base_out, halo_v, base_v, acc_v)
    go.finish()


def delta_of(loads, arr, row, before_v, slope_v):
    back = return_rows(row[...], arr[...], before_v.shape[0])
    for load in loads:
        load.wait()
    grad = (before_v[...] + back).astype(jnp.bfloat16)
    return (grad.astype(jnp.float32) * slope_v[...]).astype(jnp.bfloat16)


def backward_kernel(
    cols, arr, before, slope, row, val, ws, wn, delta_out, halo_out, base_out,
    before_v, slope_v, halo_v, base_v, acc_v, sems,
):
    go = Copies(sems)
    loads = [go.start(before, before_v), go.start(slope, slope_v)]
    delta = delta_of(loads, arr, row, before_v, slope_v)
    delta_out[...] = delta
    spread_back(go, delta, cols, val, ws, wn, halo_out, base_out, halo_v, base_v, acc_v)
    go.finish()


def final_kernel(arr, before, row, grad_out, before_v, grad_v, sems):
    go = Copies(sems)
    load = go.start(before, before_v)
    back = return_rows(row[...], arr[...], before.shape[0])
    load.wait()
    grad_v[...] = (before_v[...] + back).astype(jnp.bfloat16)
    go.store(grad_v, grad_out)
    go.finish()


def products(core, hid_v, agg_v, delta, pairs):
    for side, target in ((1 - core, pairs[0]), (core, pairs[1])):
        for n, source in enumerate((hid_v, agg_v)):

            @pl.when(side == n)
            def _(source=source, target=target):
                target[...] = mm_tn(source[...], delta).astype(jnp.bfloat16)


def weight_kernel(core, hid, agg, delta, keep, give, hid_v, agg_v, delta_v, sems):
    go = Copies(sems)
    loads = [go.start(delta, delta_v), go.start(hid, hid_v), go.start(agg, agg_v)]
    for load in loads:
        load.wait()
    products(core[0], hid_v, agg_v, delta_v[...], (give, keep))


def near_weight_kernel(core, hid, agg, delta, keep, give, sems):
    products(core[0], hid, agg, delta[...], (give, keep))


def quarters_kernel(chip, keep, got, *outs):
    size = outs[0].shape[0]
    for m, out in enumerate(outs[:-1]):
        at = pl.ds(pl.multiple_of((chip[0] ^ m) * size, size), size)
        total = keep[at, :].astype(jnp.float32) + got[at, :].astype(jnp.float32)
        out[...] = total.astype(jnp.bfloat16)


def add_kernel(scale, *refs):
    total = refs[0][...].astype(jnp.float32)
    for ref in refs[1:-2]:
        total += ref[...].astype(jnp.float32)
    if scale is not None:
        total *= scale
    refs[-2][...] = total.astype(jnp.bfloat16)


def place_kernel(layers, count, where, *refs):
    mine, other = refs[:count], refs[count : 2 * count]
    self_out, neigh_out, sems = refs[-3:]
    size = mine[0].shape[0] // len(layers)
    for core, outs in enumerate(((self_out, neigh_out), (neigh_out, self_out))):

        @pl.when(where[0] == core)
        def _(outs=outs):
            copies = []
            for m, source in enumerate((*mine, *other)):
                to = pl.multiple_of((where[1] ^ (m % count)) * size, size)
                for n, layer in enumerate(layers):
                    copies.append(
                        pltpu.make_async_copy(
                            source.at[pl.ds(n * size, size)],
                            outs[m // count].at[layer, pl.ds(to, size)],
                            sems.at[len(copies)],
                        )
                    )
            for copy in copies:
                copy.start()
            for copy in copies:
                copy.wait()


def per_device(
    features, cotangent, self_weight, neigh_weight, block_val, block_col, send_idx, send_count
):
    outer = lax.axis_size("gx")
    inner = lax.axis_size("gy")
    devices = outer * inner
    nodes, width = features.shape
    tile = block_val.shape[2]
    layers = self_weight.shape[0]
    slots = send_idx.shape[2]
    halo = devices * slots
    ext_tiles = (nodes + halo) // tile
    scale = 1.0 / math.sqrt(nodes * devices)
    bf16, f32, i32 = jnp.bfloat16, jnp.float32, jnp.int32
    near, away, scalars = pltpu.VMEM, pltpu.HBM, pltpu.SMEM

    def call(body, args, outs, scratch=(), sems=None, flops=0, alias=None):
        moved = sum(math.prod(o[0]) * jnp.dtype(o[1]).itemsize for o in outs)
        operands = [
            a if space is scalars else pltpu.with_memory_space_constraint(a, space)
            for a, space in args
        ]
        sems = len(args) + len(outs) if sems is None else sems
        return pl.pallas_call(
            body,
            in_specs=[pl.BlockSpec(memory_space=space) for _, space in args],
            out_specs=[pl.BlockSpec(memory_space=o[2]) for o in outs],
            out_shape=[o[2](o[0], o[1]) for o in outs],
            scratch_shapes=[*(pltpu.VMEM(*s) for s in scratch), pltpu.SemaphoreType.DMA((sems,))],
            input_output_aliases=alias or {},
            cost_estimate=pl.CostEstimate(
                flops=flops, bytes_accessed=2 * moved, transcendentals=0
            ),
            compiler_params=pltpu.CompilerParams(vmem_limit_bytes=16 << 20),
        )(*operands)

    rows, rows32 = ((nodes, width), bf16), ((nodes, width), f32)
    square, halo_rows = ((width, width), bf16), ((halo, width), bf16)
    ext, acc = ((ext_tiles, tile, width), bf16), ((ext_tiles, tile, width), f32)
    big = 8 * nodes * width * width

    def exchange(array):
        sent = array.reshape(devices, slots, width)
        return lax.all_to_all(sent, AXES, 0, 0, tiled=True).reshape(halo, width)

    position = lax.axis_index("gy")
    core, chip = position & 1, position >> 1
    core_arg = core.reshape(1)
    chips = inner // 2
    gx_bits = list(range(outer.bit_length() - 1))

    def flip(array, mask):
        return lax.ppermute(array, "gy", [(j, j ^ mask) for j in range(inner)])

    def flip_to(m, array):
        return flip(array, 2 * m)

    def add(*arrays, scaling=None):
        (total,) = call(
            functools.partial(add_kernel, scaling),
            [(a, near) for a in arrays],
            ((arrays[0].shape, bf16, near),),
        )
        return total

    def chip_sum(keep, give):
        got = flip(give, 1)
        mine, *others = call(
            quarters_kernel,
            ((chip.reshape(1), scalars), (keep, near), (got, near)),
            (((width // chips, width), bf16, near),) * chips,
        )
        total = add(mine, *(flip_to(m, other) for m, other in enumerate(others, 1)))
        for bit in gx_bits:
            perm = [(j, j ^ (1 << bit)) for j in range(outer)]
            got = lax.ppermute(total, "gx", perm)
            total = add(total, got, scaling=scale if bit == gx_bits[-1] else None)
        return total

    def gather(piece):
        mine, other = [piece], []
        for m in range(1, chips):
            mine.append(flip(piece, 2 * m))
        for m in range(chips):
            other.append(flip(mine[m], 1))
        return mine, other

    where = jnp.stack([core, chip]).astype(i32)

    def place(group, mine, other, outs):
        return call(
            functools.partial(place_kernel, group, chips),
            ((where, scalars), *((a, near) for a in (*mine, *other)), *((o, away) for o in outs)),
            ((self_weight.shape, bf16, away),) * 2,
            (),
            2 * chips * len(group),
            alias={1 + 2 * chips: 0, 2 + 2 * chips: 1} if outs else None,
        )

    def load(layer, *others):
        arrays = (self_weight, neigh_weight, *others)
        return call(
            functools.partial(load_kernel, layer),
            [(a, away) for a in arrays],
            [(a.shape[1:] if n < 2 else a.shape, a.dtype, near) for n, a in enumerate(arrays)],
        )

    cols = (block_col, scalars)
    row, col, send = call(
        first_kernel,
        ((send_idx.transpose(0, 2, 1), away), (send_count, away), (features, away)),
        (((1, halo), i32, near), ((halo, 1), i32, near), (*halo_rows, away)),
        (
            ((1, slots, devices), i32), ((1, devices), i32), rows, halo_rows,
        ),
    )
    arrived = exchange(send)
    ws, wn, hidden, val = load(0, features, block_val)
    hiddens, aggregates, slopes = [features], [], []
    for layer in range(layers - 1):
        aggregate, slope, kept, hidden, send = call(
            middle_kernel,
            (
                cols, (hidden, near), (arrived, near), (val, near), (ws, near), (wn, near),
                (col, near),
            ),
            ((*rows, away), (*rows32, away), (*rows, away), (*rows, near), (*halo_rows, away)),
            (ext, rows, rows32, halo_rows),
            flops=big,
        )
        hiddens.append(kept)
        aggregates.append(aggregate)
        slopes.append(slope)
        arrived = exchange(send)
        last = layer + 2 == layers
        ws, wn, *cot = load(layer + 1, *((cotangent,) if last else ()))
    aggregate, delta, outgoing, base = call(
        last_kernel,
        (
            cols, (hidden, near), (arrived, near), (val, near), (ws, near), (wn, near),
            (cot[0], near),
        ),
        ((*rows, away), (*rows, away), (*halo_rows, away), (*rows32, away)),
        (ext, rows, rows, halo_rows, rows32, acc),
        flops=2 * big,
    )
    aggregates.append(aggregate)
    sums, delta_at = [], away
    for layer in reversed(range(layers)):
        below = layer - 1
        if layer:
            sources = ((hiddens[layer], away), (aggregates[layer], away), (delta, delta_at))
        else:
            sources = ((hid, near), (agg, near), (delta, near))
        keep, give = call(
            weight_kernel if layer else near_weight_kernel,
            ((core_arg, scalars), *sources),
            ((*square, near), (*square, near)),
            (rows, rows, rows) if layer else (),
            flops=big // 2,
        )
        sums.append(chip_sum(keep, give))
        arrived = exchange(outgoing)
        if layer:
            last = (hiddens[0], aggregates[0]) if below == 0 else ()
            ws, wn, *more = load(below, *last)
            if more:
                hid, agg = more
            delta_at = near
            delta, outgoing, base = call(
                backward_kernel,
                (
                    cols, (arrived, near), (base, away), (slopes[below], away), (row, near),
                    (val, near), (ws, near), (wn, near),
                ),
                ((*rows, near), (*halo_rows, away), (*rows32, away)),
                (rows32, rows32, halo_rows, rows32, acc),
                flops=big,
            )
    (grad,) = call(
        final_kernel, ((arrived, near), (base, away), (row, near)), ((*rows, away),), (rows32, rows)
    )
    outs = ()
    for layer, piece in zip(reversed(range(layers)), sums):
        mine, other = gather(piece)
        outs = place((layer,), mine, other, outs)
    return (*outs, grad)


def solution(mesh):
    return jax.shard_map(
        per_device,
        mesh=mesh,
        in_specs=(
            P(AXES, None),
            P(AXES, None),
            P(),
            P(),
            P(AXES, None, None, None),
            P(AXES, None),
            P(AXES, None, None),
            P(AXES, None),
        ),
        out_specs=(P(), P(), P(AXES, None)),
        check_vma=False,
    )
```

```python
import functools
import math

import jax
import jax.numpy as jnp
from jax import lax
from jax.experimental import pallas as pl
from jax.experimental.pallas import tpu as pltpu
from jax.sharding import PartitionSpec as P


AXES = ("gx", "gy")


def mm(a, b):
    return jnp.dot(a, b, preferred_element_type=jnp.float32)


def mm_tn(a, b):
    return lax.dot_general(a, b, (((0,), (0,)), ((), ())), preferred_element_type=jnp.float32)


def mm_nt(a, b):
    return lax.dot_general(a, b, (((1,), (1,)), ((), ())), preferred_element_type=jnp.float32)


def iota(shape, dim):
    return lax.broadcasted_iota(jnp.int32, shape, dim)


def ones_where(mask):
    return jnp.where(mask, 1.0, 0.0).astype(jnp.bfloat16)


def pick_rows(col, table):
    hot = ones_where(iota((col.shape[0], table.shape[0]), 1) == col)
    return mm(hot, table).astype(jnp.bfloat16)


def return_rows(row, arrived, nodes):
    hot = ones_where(iota((nodes, row.shape[1]), 0) == row)
    return mm(hot, arrived)


class Copies:
    def __init__(self, sems):
        self.sems, self.used, self.stores = sems, 0, []

    def start(self, source, target):
        copy = pltpu.make_async_copy(source, target, self.sems.at[self.used])
        self.used += 1
        copy.start()
        return copy

    def store(self, source, target):
        self.stores.append(self.start(source, target))

    def finish(self):
        for copy in self.stores:
            copy.wait()


def first_kernel(idx, cnt, table, row_out, col_out, send_out, idx_v, cnt_v, table_v, send_v, sems):
    go = Copies(sems)
    loads = [go.start(idx, idx_v), go.start(cnt, cnt_v), go.start(table, table_v)]
    _, slots, peers = idx.shape
    total = peers * slots
    start_t = iota((total, peers), 1) * slots
    place_t = iota((total, peers), 0)
    inside_t = ones_where((place_t >= start_t) & (place_t < start_t + slots))
    here_t = (iota((total, slots), 0) & (slots - 1)) == iota((total, slots), 1)
    loads[0].wait()
    loads[1].wait()
    live = iota((slots, peers), 0) < jnp.broadcast_to(cnt_v[...], (slots, peers))
    code = jnp.where(live, idx_v[0] + 1, 0).astype(jnp.float32).astype(jnp.bfloat16)
    col = jnp.sum(jnp.where(here_t, mm_nt(inside_t, code), 0.0), axis=1, keepdims=True) - 1.0
    col = col.astype(jnp.int32)
    col_out[...] = col
    loads[2].wait()
    send_v[...] = pick_rows(col, table_v[...])
    go.store(send_v, send_out)
    start = iota((peers, total), 0) * slots
    place = iota((peers, total), 1)
    inside = ones_where((place >= start) & (place < start + slots))
    here = (iota((slots, total), 1) & (slots - 1)) == iota((slots, total), 0)
    row = jnp.sum(jnp.where(here, mm(code, inside), 0.0), axis=0, keepdims=True) - 1.0
    row_out[...] = row.astype(jnp.int32)
    go.finish()


def load_kernel(layer, *refs):
    count = (len(refs) - 1) // 2
    go = Copies(refs[-1])
    for n, (source, target) in enumerate(zip(refs[:count], refs[count:-1])):
        go.store(source.at[layer] if n < 2 else source, target)
    go.finish()


def pre_activation(cols, hid, arr, val, ws, wn, agg_v, ext_v):
    tiles, blocks, tile, _ = val.shape
    own = hid.shape[0] // tile
    for t in range(own):
        ext_v[t] = hid[t * tile : (t + 1) * tile, :]
    for t in range(arr.shape[0] // tile):
        ext_v[own + t] = arr[t * tile : (t + 1) * tile, :]
    for r in range(tiles):
        total = mm(val[r, 0], ext_v[cols[r, 0]])
        for b in range(1, blocks):
            total += mm(val[r, b], ext_v[cols[r, b]])
        agg_v[r * tile : (r + 1) * tile, :] = total.astype(jnp.bfloat16)
    return mm(hid[...], ws[...]) + mm(agg_v[...], wn[...])


def middle_kernel(
    cols, hid, arr, val, ws, wn, col, agg_out, slope_out, next_out, next_near, send_out,
    ext_v, agg_v, slope_v, send_v, sems,
):
    go = Copies(sems)
    pre = pre_activation(cols, hid, arr, val, ws, wn, agg_v, ext_v)
    go.store(agg_v, agg_out)
    sigma = jax.nn.sigmoid(pre)
    hidden = (pre * sigma).astype(jnp.bfloat16)
    next_near[...] = hidden
    go.store(next_near, next_out)
    slope_v[...] = sigma * (1.0 + pre * (1.0 - sigma))
    go.store(slope_v, slope_out)
    send_v[...] = pick_rows(col[...], hidden)
    go.store(send_v, send_out)
    go.finish()


def spread_back(go, delta, cols, val, ws, wn, halo_out, base_out, halo_v, base_v, acc_v):
    tiles, blocks, tile, _ = val.shape
    own = base_out.shape[0] // tile
    acc_v[...] = jnp.zeros_like(acc_v)
    upstream = mm_nt(delta, wn[...]).astype(jnp.bfloat16)
    for r in range(tiles):
        part = upstream[r * tile : (r + 1) * tile, :]
        for b in range(blocks):
            acc_v[cols[r, b]] += mm_tn(val[r, b], part)
    for t in range(halo_out.shape[0] // tile):
        halo_v[t * tile : (t + 1) * tile, :] = acc_v[own + t].astype(jnp.bfloat16)
    go.store(halo_v, halo_out)
    own_part = mm_nt(delta, ws[...])
    for t in range(own):
        at = slice(t * tile, (t + 1) * tile)
        base_v[at, :] = own_part[at, :] + acc_v[t]
    go.store(base_v, base_out)


def last_kernel(
    cols, hid, arr, val, ws, wn, cot, agg_out, delta_out, halo_out, base_out,
    ext_v, agg_v, delta_v, halo_v, base_v, acc_v, sems,
):
    go = Copies(sems)
    pre = pre_activation(cols, hid, arr, val, ws, wn, agg_v, ext_v)
    go.store(agg_v, agg_out)
    sigma = jax.nn.sigmoid(pre)
    slope = sigma * (1.0 + pre * (1.0 - sigma))
    delta = (cot[...].astype(jnp.float32) * slope).astype(jnp.bfloat16)
    delta_v[...] = delta
    go.store(delta_v, delta_out)
    spread_back(go, delta, cols, val, ws, wn, halo_out, base_out, halo_v, base_v, acc_v)
    go.finish()


def delta_of(loads, arr, row, before_v, slope_v):
    back = return_rows(row[...], arr[...], before_v.shape[0])
    for load in loads:
        load.wait()
    grad = (before_v[...] + back).astype(jnp.bfloat16)
    return (grad.astype(jnp.float32) * slope_v[...]).astype(jnp.bfloat16)


def backward_kernel(
    cols, arr, before, slope, row, val, ws, wn, delta_out, halo_out, base_out,
    before_v, slope_v, halo_v, base_v, acc_v, sems,
):
    go = Copies(sems)
    loads = [go.start(before, before_v), go.start(slope, slope_v)]
    delta = delta_of(loads, arr, row, before_v, slope_v)
    delta_out[...] = delta
    spread_back(go, delta, cols, val, ws, wn, halo_out, base_out, halo_v, base_v, acc_v)
    go.finish()


def top_kernel(
    core, hid, agg, arr, before, slope, row, delta_out, keep, give, before_v, slope_v, sems
):
    go = Copies(sems)
    loads = [go.start(before, before_v), go.start(slope, slope_v)]
    delta = delta_of(loads, arr, row, before_v, slope_v)
    delta_out[...] = delta
    products(core[0], hid, agg, delta, (give, keep))


def spread_kernel(cols, delta, val, ws, wn, halo_out, base_out, halo_v, base_v, acc_v, sems):
    go = Copies(sems)
    spread_back(go, delta[...], cols, val, ws, wn, halo_out, base_out, halo_v, base_v, acc_v)
    go.finish()


def final_kernel(arr, before, row, grad_out, before_v, grad_v, sems):
    go = Copies(sems)
    load = go.start(before, before_v)
    back = return_rows(row[...], arr[...], before.shape[0])
    load.wait()
    grad_v[...] = (before_v[...] + back).astype(jnp.bfloat16)
    go.store(grad_v, grad_out)
    go.finish()


def products(core, hid_v, agg_v, delta, pairs):
    for side, target in ((1 - core, pairs[0]), (core, pairs[1])):
        for n, source in enumerate((hid_v, agg_v)):

            @pl.when(side == n)
            def _(source=source, target=target):
                target[...] = mm_tn(source[...], delta).astype(jnp.bfloat16)


def weight_kernel(core, hid, agg, delta, keep, give, hid_v, agg_v, delta_v, sems):
    go = Copies(sems)
    loads = [go.start(delta, delta_v), go.start(hid, hid_v), go.start(agg, agg_v)]
    for load in loads:
        load.wait()
    products(core[0], hid_v, agg_v, delta_v[...], (give, keep))


def quarters_kernel(chip, keep, got, *outs):
    size = outs[0].shape[0]
    for m, out in enumerate(outs[:-1]):
        at = pl.ds(pl.multiple_of((chip[0] ^ m) * size, size), size)
        total = keep[at, :].astype(jnp.float32) + got[at, :].astype(jnp.float32)
        out[...] = total.astype(jnp.bfloat16)


def add_kernel(scale, *refs):
    total = refs[0][...].astype(jnp.float32)
    for ref in refs[1:-2]:
        total += ref[...].astype(jnp.float32)
    if scale is not None:
        total *= scale
    refs[-2][...] = total.astype(jnp.bfloat16)


def place_kernel(layers, count, where, *refs):
    mine, other = refs[:count], refs[count : 2 * count]
    self_out, neigh_out, sems = refs[-3:]
    size = mine[0].shape[0] // len(layers)
    for core, outs in enumerate(((self_out, neigh_out), (neigh_out, self_out))):

        @pl.when(where[0] == core)
        def _(outs=outs):
            copies = []
            for m, source in enumerate((*mine, *other)):
                to = pl.multiple_of((where[1] ^ (m % count)) * size, size)
                for n, layer in enumerate(layers):
                    copies.append(
                        pltpu.make_async_copy(
                            source.at[pl.ds(n * size, size)],
                            outs[m // count].at[layer, pl.ds(to, size)],
                            sems.at[len(copies)],
                        )
                    )
            for copy in copies:
                copy.start()
            for copy in copies:
                copy.wait()


def per_device(
    features, cotangent, self_weight, neigh_weight, block_val, block_col, send_idx, send_count
):
    outer = lax.axis_size("gx")
    inner = lax.axis_size("gy")
    devices = outer * inner
    nodes, width = features.shape
    tile = block_val.shape[2]
    layers = self_weight.shape[0]
    slots = send_idx.shape[2]
    halo = devices * slots
    ext_tiles = (nodes + halo) // tile
    scale = 1.0 / math.sqrt(nodes * devices)
    bf16, f32, i32 = jnp.bfloat16, jnp.float32, jnp.int32
    near, away, scalars = pltpu.VMEM, pltpu.HBM, pltpu.SMEM

    def call(body, args, outs, scratch=(), sems=None, flops=0, alias=None):
        moved = sum(math.prod(o[0]) * jnp.dtype(o[1]).itemsize for o in outs)
        operands = [
            a if space is scalars else pltpu.with_memory_space_constraint(a, space)
            for a, space in args
        ]
        sems = len(args) + len(outs) if sems is None else sems
        return pl.pallas_call(
            body,
            in_specs=[pl.BlockSpec(memory_space=space) for _, space in args],
            out_specs=[pl.BlockSpec(memory_space=o[2]) for o in outs],
            out_shape=[o[2](o[0], o[1]) for o in outs],
            scratch_shapes=[*(pltpu.VMEM(*s) for s in scratch), pltpu.SemaphoreType.DMA((sems,))],
            input_output_aliases=alias or {},
            cost_estimate=pl.CostEstimate(
                flops=flops, bytes_accessed=2 * moved, transcendentals=0
            ),
            compiler_params=pltpu.CompilerParams(vmem_limit_bytes=16 << 20),
        )(*operands)

    rows, rows32 = ((nodes, width), bf16), ((nodes, width), f32)
    square, halo_rows = ((width, width), bf16), ((halo, width), bf16)
    ext, acc = ((ext_tiles, tile, width), bf16), ((ext_tiles, tile, width), f32)
    big = 8 * nodes * width * width

    def exchange(array):
        sent = array.reshape(devices, slots, width)
        return lax.all_to_all(sent, AXES, 0, 0, tiled=True).reshape(halo, width)

    position = lax.axis_index("gy")
    core, chip = position & 1, position >> 1
    core_arg = core.reshape(1)
    chips = inner // 2
    gx_bits = list(range(outer.bit_length() - 1))

    def flip(array, mask):
        return lax.ppermute(array, "gy", [(j, j ^ mask) for j in range(inner)])

    def flip_to(m, array):
        return flip(array, 2 * m)

    def add(*arrays, scaling=None):
        (total,) = call(
            functools.partial(add_kernel, scaling),
            [(a, near) for a in arrays],
            ((arrays[0].shape, bf16, near),),
        )
        return total

    def chip_sum(keep, give):
        got = flip(give, 1)
        mine, *others = call(
            quarters_kernel,
            ((chip.reshape(1), scalars), (keep, near), (got, near)),
            (((width // chips, width), bf16, near),) * chips,
        )
        total = add(mine, *(flip_to(m, other) for m, other in enumerate(others, 1)))
        for bit in gx_bits:
            perm = [(j, j ^ (1 << bit)) for j in range(outer)]
            got = lax.ppermute(total, "gx", perm)
            total = add(total, got, scaling=scale if bit == gx_bits[-1] else None)
        return total

    def gather(piece):
        mine, other = [piece], []
        for m in range(1, chips):
            mine.append(flip(piece, 2 * m))
        for m in range(chips):
            other.append(flip(mine[m], 1))
        return mine, other

    where = jnp.stack([core, chip]).astype(i32)

    def place(group, mine, other, outs):
        return call(
            functools.partial(place_kernel, group, chips),
            ((where, scalars), *((a, near) for a in (*mine, *other)), *((o, away) for o in outs)),
            ((self_weight.shape, bf16, away),) * 2,
            (),
            2 * chips * len(group),
            alias={1 + 2 * chips: 0, 2 + 2 * chips: 1} if outs else None,
        )

    def load(layer, *others):
        arrays = (self_weight, neigh_weight, *others)
        return call(
            functools.partial(load_kernel, layer),
            [(a, away) for a in arrays],
            [(a.shape[1:] if n < 2 else a.shape, a.dtype, near) for n, a in enumerate(arrays)],
        )

    cols = (block_col, scalars)
    row, col, send = call(
        first_kernel,
        ((send_idx.transpose(0, 2, 1), away), (send_count, away), (features, away)),
        (((1, halo), i32, near), ((halo, 1), i32, near), (*halo_rows, away)),
        (
            ((1, slots, devices), i32), ((1, devices), i32), rows, halo_rows,
        ),
    )
    arrived = exchange(send)
    ws, wn, hidden, val = load(0, features, block_val)
    hiddens, aggregates, slopes = [features], [], []
    for layer in range(layers - 1):
        aggregate, slope, kept, hidden, send = call(
            middle_kernel,
            (
                cols, (hidden, near), (arrived, near), (val, near), (ws, near), (wn, near),
                (col, near),
            ),
            ((*rows, away), (*rows32, away), (*rows, away), (*rows, near), (*halo_rows, away)),
            (ext, rows, rows32, halo_rows),
            flops=big,
        )
        hiddens.append(kept)
        aggregates.append(aggregate)
        slopes.append(slope)
        arrived = exchange(send)
        last = layer + 2 == layers
        ws, wn, *cot = load(layer + 1, *((cotangent,) if last else ()))
    aggregate, delta, outgoing, base = call(
        last_kernel,
        (
            cols, (hidden, near), (arrived, near), (val, near), (ws, near), (wn, near),
            (cot[0], near),
        ),
        ((*rows, away), (*rows, away), (*halo_rows, away), (*rows32, away)),
        (ext, rows, rows, halo_rows, rows32, acc),
        flops=2 * big,
    )
    aggregates.append(aggregate)
    sums, delta_at = [], away
    for layer in reversed(range(layers)):
        below = layer - 1
        if layer:
            keep, give = call(
                weight_kernel,
                (
                    (core_arg, scalars), (hiddens[layer], away), (aggregates[layer], away),
                    (delta, delta_at),
                ),
                ((*square, near), (*square, near)),
                (rows, rows, rows),
                flops=big // 2,
            )
        sums.append(chip_sum(keep, give))
        arrived = exchange(outgoing)
        if not layer:
            break
        last = (hiddens[0], aggregates[0]) if below == 0 else ()
        ws, wn, *more = load(below, *last)
        back = ((arrived, near), (base, away), (slopes[below], away), (row, near))
        graph = ((val, near), (ws, near), (wn, near))
        delta_at = near
        if below:
            delta, outgoing, base = call(
                backward_kernel,
                (cols, *back, *graph),
                ((*rows, near), (*halo_rows, away), (*rows32, away)),
                (rows32, rows32, halo_rows, rows32, acc),
                flops=big,
            )
        else:
            delta, keep, give = call(
                top_kernel,
                ((core_arg, scalars), *((a, near) for a in more), *back),
                ((*rows, near), (*square, near), (*square, near)),
                (rows32, rows32),
                flops=big,
            )
        if not below:
            outgoing, base = call(
                spread_kernel,
                (cols, (delta, near), *graph),
                ((*halo_rows, away), (*rows32, away)),
                (halo_rows, rows32, acc),
                flops=big,
            )
    (grad,) = call(
        final_kernel, ((arrived, near), (base, away), (row, near)), ((*rows, away),), (rows32, rows)
    )
    outs = ()
    for layer, piece in zip(reversed(range(layers)), sums):
        mine, other = gather(piece)
        outs = place((layer,), mine, other, outs)
    return (*outs, grad)


def solution(mesh):
    return jax.shard_map(
        per_device,
        mesh=mesh,
        in_specs=(
            P(AXES, None),
            P(AXES, None),
            P(),
            P(),
            P(AXES, None, None, None),
            P(AXES, None),
            P(AXES, None, None),
            P(AXES, None),
        ),
        out_specs=(P(), P(), P(AXES, None)),
        check_vma=False,
    )
```

```python
import functools
import math

import jax
import jax.numpy as jnp
from jax import lax
from jax.experimental import pallas as pl
from jax.experimental.pallas import tpu as pltpu
from jax.sharding import PartitionSpec as P


AXES = ("gx", "gy")


def mm(a, b):
    return jnp.dot(a, b, preferred_element_type=jnp.float32)


def mm_tn(a, b):
    return lax.dot_general(a, b, (((0,), (0,)), ((), ())), preferred_element_type=jnp.float32)


def mm_nt(a, b):
    return lax.dot_general(a, b, (((1,), (1,)), ((), ())), preferred_element_type=jnp.float32)


def iota(shape, dim):
    return lax.broadcasted_iota(jnp.int32, shape, dim)


def ones_where(mask):
    return jnp.where(mask, 1.0, 0.0).astype(jnp.bfloat16)


def pick_rows(col, table):
    hot = ones_where(iota((col.shape[0], table.shape[0]), 1) == col)
    return mm(hot, table).astype(jnp.bfloat16)


def return_rows(row, arrived, nodes):
    hot = ones_where(iota((nodes, row.shape[1]), 0) == row)
    return mm(hot, arrived)


class Copies:
    def __init__(self, sems):
        self.sems, self.used, self.stores = sems, 0, []

    def start(self, source, target):
        copy = pltpu.make_async_copy(source, target, self.sems.at[self.used])
        self.used += 1
        copy.start()
        return copy

    def store(self, source, target):
        self.stores.append(self.start(source, target))

    def finish(self):
        for copy in self.stores:
            copy.wait()


def first_kernel(idx, cnt, table, row_out, col_out, send_out, idx_v, cnt_v, table_v, send_v, sems):
    go = Copies(sems)
    loads = [go.start(idx, idx_v), go.start(cnt, cnt_v), go.start(table, table_v)]
    _, slots, peers = idx.shape
    total = peers * slots
    start_t = iota((total, peers), 1) * slots
    place_t = iota((total, peers), 0)
    inside_t = ones_where((place_t >= start_t) & (place_t < start_t + slots))
    here_t = (iota((total, slots), 0) & (slots - 1)) == iota((total, slots), 1)
    loads[0].wait()
    loads[1].wait()
    live = iota((slots, peers), 0) < jnp.broadcast_to(cnt_v[...], (slots, peers))
    code = jnp.where(live, idx_v[0] + 1, 0).astype(jnp.float32).astype(jnp.bfloat16)
    col = jnp.sum(jnp.where(here_t, mm_nt(inside_t, code), 0.0), axis=1, keepdims=True) - 1.0
    col = col.astype(jnp.int32)
    col_out[...] = col
    loads[2].wait()
    send_v[...] = pick_rows(col, table_v[...])
    go.store(send_v, send_out)
    start = iota((peers, total), 0) * slots
    place = iota((peers, total), 1)
    inside = ones_where((place >= start) & (place < start + slots))
    here = (iota((slots, total), 1) & (slots - 1)) == iota((slots, total), 0)
    row = jnp.sum(jnp.where(here, mm(code, inside), 0.0), axis=0, keepdims=True) - 1.0
    row_out[...] = row.astype(jnp.int32)
    go.finish()


def load_kernel(layer, *refs):
    count = (len(refs) - 1) // 2
    go = Copies(refs[-1])
    for source, target in zip(refs[:count], refs[count:-1]):
        go.store(source if source.shape == target.shape else source.at[layer], target)
    go.finish()


def pre_activation(cols, hid, arr, val, ws, wn, agg_v, ext_v):
    tiles, blocks, tile, _ = val.shape
    own = hid.shape[0] // tile
    for t in range(own):
        ext_v[t] = hid[t * tile : (t + 1) * tile, :]
    for t in range(arr.shape[0] // tile):
        ext_v[own + t] = arr[t * tile : (t + 1) * tile, :]
    for r in range(tiles):
        total = mm(val[r, 0], ext_v[cols[r, 0]])
        for b in range(1, blocks):
            total += mm(val[r, b], ext_v[cols[r, b]])
        agg_v[r * tile : (r + 1) * tile, :] = total.astype(jnp.bfloat16)
    return mm(hid[...], ws[...]) + mm(agg_v[...], wn[...])


def middle_kernel(
    cols, hid, arr, val, ws, wn, col, agg_out, slope_out, next_out, next_near, send_out,
    ext_v, agg_v, slope_v, send_v, sems,
):
    go = Copies(sems)
    pre = pre_activation(cols, hid, arr, val, ws, wn, agg_v, ext_v)
    go.store(agg_v, agg_out)
    sigma = jax.nn.sigmoid(pre)
    hidden = (pre * sigma).astype(jnp.bfloat16)
    next_near[...] = hidden
    go.store(next_near, next_out)
    slope_v[...] = sigma * (1.0 + pre * (1.0 - sigma))
    go.store(slope_v, slope_out)
    send_v[...] = pick_rows(col[...], hidden)
    go.store(send_v, send_out)
    go.finish()


def spread_back(go, delta, cols, val, ws, wn, halo_out, base_out, halo_v, base_v, acc_v):
    tiles, blocks, tile, _ = val.shape
    own = base_out.shape[0] // tile
    acc_v[...] = jnp.zeros_like(acc_v)
    upstream = mm_nt(delta, wn[...]).astype(jnp.bfloat16)
    for r in range(tiles):
        part = upstream[r * tile : (r + 1) * tile, :]
        for b in range(blocks):
            acc_v[cols[r, b]] += mm_tn(val[r, b], part)
    for t in range(halo_out.shape[0] // tile):
        halo_v[t * tile : (t + 1) * tile, :] = acc_v[own + t].astype(jnp.bfloat16)
    go.store(halo_v, halo_out)
    own_part = mm_nt(delta, ws[...])
    for t in range(own):
        at = slice(t * tile, (t + 1) * tile)
        base_v[at, :] = own_part[at, :] + acc_v[t]
    go.store(base_v, base_out)


def last_kernel(
    cols, hid, arr, val, ws, wn, cot, agg_out, delta_out, halo_out, base_out,
    ext_v, agg_v, delta_v, halo_v, base_v, acc_v, sems,
):
    go = Copies(sems)
    pre = pre_activation(cols, hid, arr, val, ws, wn, agg_v, ext_v)
    go.store(agg_v, agg_out)
    sigma = jax.nn.sigmoid(pre)
    slope = sigma * (1.0 + pre * (1.0 - sigma))
    delta = (cot[...].astype(jnp.float32) * slope).astype(jnp.bfloat16)
    delta_v[...] = delta
    go.store(delta_v, delta_out)
    spread_back(go, delta, cols, val, ws, wn, halo_out, base_out, halo_v, base_v, acc_v)
    go.finish()


def delta_of(arr, before, slope, row):
    back = return_rows(row[...], arr[...], before.shape[0])
    grad = (before[...] + back).astype(jnp.bfloat16)
    return (grad.astype(jnp.float32) * slope[...]).astype(jnp.bfloat16)


def backward_kernel(
    cols, arr, before, slope, row, val, ws, wn, delta_out, halo_out, base_out,
    delta_v, halo_v, base_v, acc_v, sems,
):
    go = Copies(sems)
    delta = delta_of(arr, before, slope, row)
    delta_v[...] = delta
    go.store(delta_v, delta_out)
    spread_back(go, delta, cols, val, ws, wn, halo_out, base_out, halo_v, base_v, acc_v)
    go.finish()


def top_kernel(core, hid, agg, arr, before, slope, row, delta_out, keep, give, sems):
    delta = delta_of(arr, before, slope, row)
    delta_out[...] = delta
    products(core[0], hid, agg, delta, (give, keep))


def spread_kernel(
    layer, cols, delta, val, ws, wn, halo_out, base_out, ws_v, wn_v, halo_v, base_v, acc_v, sems
):
    go = Copies(sems)
    for load in (go.start(wn.at[layer], wn_v), go.start(ws.at[layer], ws_v)):
        load.wait()
    spread_back(go, delta[...], cols, val, ws_v, wn_v, halo_out, base_out, halo_v, base_v, acc_v)
    go.finish()


def final_kernel(arr, before, row, grad_out, before_v, grad_v, sems):
    go = Copies(sems)
    load = go.start(before, before_v)
    back = return_rows(row[...], arr[...], before.shape[0])
    load.wait()
    grad_v[...] = (before_v[...] + back).astype(jnp.bfloat16)
    go.store(grad_v, grad_out)
    go.finish()


def products(core, hid_v, agg_v, delta, pairs):
    for side, target in ((1 - core, pairs[0]), (core, pairs[1])):
        for n, source in enumerate((hid_v, agg_v)):

            @pl.when(side == n)
            def _(source=source, target=target):
                target[...] = mm_tn(source[...], delta).astype(jnp.bfloat16)


def weight_kernel(core, hid, agg, delta, keep, give, hid_v, agg_v, delta_v, sems):
    go = Copies(sems)
    loads = [go.start(delta, delta_v), go.start(hid, hid_v), go.start(agg, agg_v)]
    for load in loads:
        load.wait()
    products(core[0], hid_v, agg_v, delta_v[...], (give, keep))


def quarters_kernel(chip, keep, got, *outs):
    size = outs[0].shape[0]
    for m, out in enumerate(outs[:-1]):
        at = pl.ds(pl.multiple_of((chip[0] ^ m) * size, size), size)
        total = keep[at, :].astype(jnp.float32) + got[at, :].astype(jnp.float32)
        out[...] = total.astype(jnp.bfloat16)


def add_kernel(scale, *refs):
    total = refs[0][...].astype(jnp.float32)
    for ref in refs[1:-2]:
        total += ref[...].astype(jnp.float32)
    if scale is not None:
        total *= scale
    refs[-2][...] = total.astype(jnp.bfloat16)


def place_kernel(layers, count, where, *refs):
    mine, other = refs[:count], refs[count : 2 * count]
    self_out, neigh_out, sems = refs[-3:]
    size = mine[0].shape[0] // len(layers)
    for core, outs in enumerate(((self_out, neigh_out), (neigh_out, self_out))):

        @pl.when(where[0] == core)
        def _(outs=outs):
            copies = []
            for m, source in enumerate((*mine, *other)):
                to = pl.multiple_of((where[1] ^ (m % count)) * size, size)
                for n, layer in enumerate(layers):
                    copies.append(
                        pltpu.make_async_copy(
                            source.at[pl.ds(n * size, size)],
                            outs[m // count].at[layer, pl.ds(to, size)],
                            sems.at[len(copies)],
                        )
                    )
            for copy in copies:
                copy.start()
            for copy in copies:
                copy.wait()


def per_device(
    features, cotangent, self_weight, neigh_weight, block_val, block_col, send_idx, send_count
):
    outer = lax.axis_size("gx")
    inner = lax.axis_size("gy")
    devices = outer * inner
    nodes, width = features.shape
    tile = block_val.shape[2]
    layers = self_weight.shape[0]
    slots = send_idx.shape[2]
    halo = devices * slots
    ext_tiles = (nodes + halo) // tile
    scale = 1.0 / math.sqrt(nodes * devices)
    bf16, f32, i32 = jnp.bfloat16, jnp.float32, jnp.int32
    near, away, scalars = pltpu.VMEM, pltpu.HBM, pltpu.SMEM

    def call(body, args, outs, scratch=(), sems=None, flops=0, alias=None):
        moved = sum(math.prod(o[0]) * jnp.dtype(o[1]).itemsize for o in outs)
        operands = [
            a if space is scalars else pltpu.with_memory_space_constraint(a, space)
            for a, space in args
        ]
        sems = len(args) + len(outs) if sems is None else sems
        return pl.pallas_call(
            body,
            in_specs=[pl.BlockSpec(memory_space=space) for _, space in args],
            out_specs=[pl.BlockSpec(memory_space=o[2]) for o in outs],
            out_shape=[o[2](o[0], o[1]) for o in outs],
            scratch_shapes=[*(pltpu.VMEM(*s) for s in scratch), pltpu.SemaphoreType.DMA((sems,))],
            input_output_aliases=alias or {},
            cost_estimate=pl.CostEstimate(
                flops=flops, bytes_accessed=2 * moved, transcendentals=0
            ),
            compiler_params=pltpu.CompilerParams(vmem_limit_bytes=16 << 20),
        )(*operands)

    rows, rows32 = ((nodes, width), bf16), ((nodes, width), f32)
    square, halo_rows = ((width, width), bf16), ((halo, width), bf16)
    ext, acc = ((ext_tiles, tile, width), bf16), ((ext_tiles, tile, width), f32)
    big = 8 * nodes * width * width

    def exchange(array):
        sent = array.reshape(devices, slots, width)
        return lax.all_to_all(sent, AXES, 0, 0, tiled=True).reshape(halo, width)

    position = lax.axis_index("gy")
    core, chip = position & 1, position >> 1
    core_arg = core.reshape(1)
    chips = inner // 2
    gx_bits = list(range(outer.bit_length() - 1))

    def flip(array, mask):
        return lax.ppermute(array, "gy", [(j, j ^ mask) for j in range(inner)])

    def flip_to(m, array):
        return flip(array, 2 * m)

    def add(*arrays, scaling=None):
        (total,) = call(
            functools.partial(add_kernel, scaling),
            [(a, near) for a in arrays],
            ((arrays[0].shape, bf16, near),),
        )
        return total

    def chip_sum(keep, give):
        got = flip(give, 1)
        mine, *others = call(
            quarters_kernel,
            ((chip.reshape(1), scalars), (keep, near), (got, near)),
            (((width // chips, width), bf16, near),) * chips,
        )
        total = add(mine, *(flip_to(m, other) for m, other in enumerate(others, 1)))
        for bit in gx_bits:
            perm = [(j, j ^ (1 << bit)) for j in range(outer)]
            got = lax.ppermute(total, "gx", perm)
            total = add(total, got, scaling=scale if bit == gx_bits[-1] else None)
        return total

    def gather(piece):
        mine, other = [piece], []
        for m in range(1, chips):
            mine.append(flip(piece, 2 * m))
        for m in range(chips):
            other.append(flip(mine[m], 1))
        return mine, other

    where = jnp.stack([core, chip]).astype(i32)

    def place(group, mine, other, outs):
        return call(
            functools.partial(place_kernel, group, chips),
            ((where, scalars), *((a, near) for a in (*mine, *other)), *((o, away) for o in outs)),
            ((self_weight.shape, bf16, away),) * 2,
            (),
            2 * chips * len(group),
            alias={1 + 2 * chips: 0, 2 + 2 * chips: 1} if outs else None,
        )

    weights = (self_weight, neigh_weight)

    def load(layer, *arrays):
        return call(
            functools.partial(load_kernel, layer),
            [(a, away) for a in arrays],
            [
                (a.shape[1:] if a is self_weight or a is neigh_weight else a.shape, a.dtype, near)
                for a in arrays
            ],
        )

    cols = (block_col, scalars)
    row, col, send = call(
        first_kernel,
        ((send_idx.transpose(0, 2, 1), away), (send_count, away), (features, away)),
        (((1, halo), i32, near), ((halo, 1), i32, near), (*halo_rows, away)),
        (
            ((1, slots, devices), i32), ((1, devices), i32), rows, halo_rows,
        ),
    )
    arrived = exchange(send)
    ws, wn, hidden, val = load(0, *weights, features, block_val)
    hiddens, aggregates, slopes = [features], [], []
    for layer in range(layers - 1):
        aggregate, slope, kept, hidden, send = call(
            middle_kernel,
            (
                cols, (hidden, near), (arrived, near), (val, near), (ws, near), (wn, near),
                (col, near),
            ),
            ((*rows, away), (*rows32, away), (*rows, away), (*rows, near), (*halo_rows, away)),
            (ext, rows, rows32, halo_rows),
            flops=big,
        )
        hiddens.append(kept)
        aggregates.append(aggregate)
        slopes.append(slope)
        arrived = exchange(send)
        last = layer + 2 == layers
        ws, wn, *cot = load(layer + 1, *weights, *((cotangent,) if last else ()))
    aggregate, delta, outgoing, base = call(
        last_kernel,
        (
            cols, (hidden, near), (arrived, near), (val, near), (ws, near), (wn, near),
            (cot[0], near),
        ),
        ((*rows, away), (*rows, away), (*halo_rows, away), (*rows32, away)),
        (ext, rows, rows, halo_rows, rows32, acc),
        flops=2 * big,
    )
    aggregates.append(aggregate)
    sums = []
    for layer in reversed(range(layers)):
        below = layer - 1
        if layer:
            keep, give = call(
                weight_kernel,
                (
                    (core_arg, scalars), (hiddens[layer], away), (aggregates[layer], away),
                    (delta, away),
                ),
                ((*square, near), (*square, near)),
                (rows, rows, rows),
                flops=big // 2,
            )
        sums.append(chip_sum(keep, give))
        arrived = exchange(outgoing)
        if not layer:
            break
        more = weights if below else (hiddens[0], aggregates[0])
        base, slope, *more = load(below, base, slopes[below], *more)
        back = ((arrived, near), (base, near), (slope, near), (row, near))
        if below:
            delta, outgoing, base = call(
                backward_kernel,
                (cols, *back, (val, near), *((a, near) for a in more)),
                ((*rows, away), (*halo_rows, away), (*rows32, away)),
                (rows, halo_rows, rows32, acc),
                flops=big,
            )
        else:
            delta, keep, give = call(
                top_kernel,
                ((core_arg, scalars), *((a, near) for a in more), *back),
                ((*rows, near), (*square, near), (*square, near)),
                flops=big,
            )
        if not below:
            outgoing, base = call(
                functools.partial(spread_kernel, 0),
                (cols, (delta, near), (val, near), *((w, away) for w in weights)),
                ((*halo_rows, away), (*rows32, away)),
                (square, square, halo_rows, rows32, acc),
                flops=big,
            )
    (grad,) = call(
        final_kernel, ((arrived, near), (base, away), (row, near)), ((*rows, away),), (rows32, rows)
    )
    outs = ()
    for layer, piece in zip(reversed(range(layers)), sums):
        mine, other = gather(piece)
        outs = place((layer,), mine, other, outs)
    return (*outs, grad)


def solution(mesh):
    return jax.shard_map(
        per_device,
        mesh=mesh,
        in_specs=(
            P(AXES, None),
            P(AXES, None),
            P(),
            P(),
            P(AXES, None, None, None),
            P(AXES, None),
            P(AXES, None, None),
            P(AXES, None),
        ),
        out_specs=(P(), P(), P(AXES, None)),
        check_vma=False,
    )
```

```python
import functools
import math

import jax
import jax.numpy as jnp
from jax import lax
from jax.experimental import pallas as pl
from jax.experimental.pallas import tpu as pltpu
from jax.sharding import PartitionSpec as P


AXES = ("gx", "gy")


def mm(a, b):
    return jnp.dot(a, b, preferred_element_type=jnp.float32)


def mm_tn(a, b):
    return lax.dot_general(a, b, (((0,), (0,)), ((), ())), preferred_element_type=jnp.float32)


def mm_nt(a, b):
    return lax.dot_general(a, b, (((1,), (1,)), ((), ())), preferred_element_type=jnp.float32)


def iota(shape, dim):
    return lax.broadcasted_iota(jnp.int32, shape, dim)


def ones_where(mask):
    return jnp.where(mask, 1.0, 0.0).astype(jnp.bfloat16)


def pick_rows(col, table):
    hot = ones_where(iota((col.shape[0], table.shape[0]), 1) == col)
    return mm(hot, table).astype(jnp.bfloat16)


def return_rows(row, arrived, nodes):
    hot = ones_where(iota((nodes, row.shape[1]), 0) == row)
    return mm(hot, arrived)


class Copies:
    def __init__(self, sems):
        self.sems, self.used, self.stores = sems, 0, []

    def start(self, source, target):
        copy = pltpu.make_async_copy(source, target, self.sems.at[self.used])
        self.used += 1
        copy.start()
        return copy

    def store(self, source, target):
        self.stores.append(self.start(source, target))

    def finish(self):
        for copy in self.stores:
            copy.wait()


def first_kernel(idx, cnt, table, row_out, col_out, send_out, idx_v, cnt_v, table_v, send_v, sems):
    go = Copies(sems)
    loads = [go.start(idx, idx_v), go.start(cnt, cnt_v), go.start(table, table_v)]
    _, slots, peers = idx.shape
    total = peers * slots
    start_t = iota((total, peers), 1) * slots
    place_t = iota((total, peers), 0)
    inside_t = ones_where((place_t >= start_t) & (place_t < start_t + slots))
    here_t = (iota((total, slots), 0) & (slots - 1)) == iota((total, slots), 1)
    loads[0].wait()
    loads[1].wait()
    live = iota((slots, peers), 0) < jnp.broadcast_to(cnt_v[...], (slots, peers))
    code = jnp.where(live, idx_v[0] + 1, 0).astype(jnp.float32).astype(jnp.bfloat16)
    col = jnp.sum(jnp.where(here_t, mm_nt(inside_t, code), 0.0), axis=1, keepdims=True) - 1.0
    col = col.astype(jnp.int32)
    col_out[...] = col
    loads[2].wait()
    send_v[...] = pick_rows(col, table_v[...])
    go.store(send_v, send_out)
    start = iota((peers, total), 0) * slots
    place = iota((peers, total), 1)
    inside = ones_where((place >= start) & (place < start + slots))
    here = (iota((slots, total), 1) & (slots - 1)) == iota((slots, total), 0)
    row = jnp.sum(jnp.where(here, mm(code, inside), 0.0), axis=0, keepdims=True) - 1.0
    row_out[...] = row.astype(jnp.int32)
    go.finish()


def load_kernel(layer, *refs):
    count = (len(refs) - 1) // 2
    go = Copies(refs[-1])
    for source, target in zip(refs[:count], refs[count:-1]):
        go.store(source if source.shape == target.shape else source.at[layer], target)
    go.finish()


def pre_activation(cols, hid, arr, val, ws, wn, agg_v, ext_v):
    tiles, blocks, tile, _ = val.shape
    own = hid.shape[0] // tile
    for t in range(own):
        ext_v[t] = hid[t * tile : (t + 1) * tile, :]
    for t in range(arr.shape[0] // tile):
        ext_v[own + t] = arr[t * tile : (t + 1) * tile, :]
    for r in range(tiles):
        total = mm(val[r, 0], ext_v[cols[r, 0]])
        for b in range(1, blocks):
            total += mm(val[r, b], ext_v[cols[r, b]])
        agg_v[r * tile : (r + 1) * tile, :] = total.astype(jnp.bfloat16)
    return mm(hid[...], ws[...]) + mm(agg_v[...], wn[...])


def middle_kernel(
    cols, hid, arr, val, ws, wn, col, agg_out, slope_out, next_out, next_near, send_out,
    ext_v, agg_v, slope_v, send_v, sems,
):
    go = Copies(sems)
    pre = pre_activation(cols, hid, arr, val, ws, wn, agg_v, ext_v)
    go.store(agg_v, agg_out)
    sigma = jax.nn.sigmoid(pre)
    hidden = (pre * sigma).astype(jnp.bfloat16)
    next_near[...] = hidden
    go.store(next_near, next_out)
    slope_v[...] = sigma * (1.0 + pre * (1.0 - sigma))
    go.store(slope_v, slope_out)
    send_v[...] = pick_rows(col[...], hidden)
    go.store(send_v, send_out)
    go.finish()


def spread_back(go, delta, cols, val, ws, wn, halo_out, base, halo_v, acc_v, ready=None):
    tiles, blocks, tile, _ = val.shape
    own = base.shape[0] // tile
    acc_v[...] = jnp.zeros_like(acc_v)
    upstream = mm_nt(delta, wn[...]).astype(jnp.bfloat16)
    for r in range(tiles):
        part = upstream[r * tile : (r + 1) * tile, :]
        for b in range(blocks):
            acc_v[cols[r, b]] += mm_tn(val[r, b], part)
    for t in range(halo_out.shape[0] // tile):
        halo_v[t * tile : (t + 1) * tile, :] = acc_v[own + t].astype(jnp.bfloat16)
    go.store(halo_v, halo_out)
    if ready is not None:
        ready.wait()
    own_part = mm_nt(delta, ws[...])
    for t in range(own):
        at = slice(t * tile, (t + 1) * tile)
        base[at, :] = own_part[at, :] + acc_v[t]


def last_kernel(
    cols, hid, arr, val, ws, wn, cot, agg_out, delta_out, halo_out, base_out,
    ext_v, agg_v, delta_v, halo_v, base_v, acc_v, sems,
):
    go = Copies(sems)
    pre = pre_activation(cols, hid, arr, val, ws, wn, agg_v, ext_v)
    go.store(agg_v, agg_out)
    sigma = jax.nn.sigmoid(pre)
    slope = sigma * (1.0 + pre * (1.0 - sigma))
    delta = (cot[...].astype(jnp.float32) * slope).astype(jnp.bfloat16)
    delta_v[...] = delta
    go.store(delta_v, delta_out)
    spread_back(go, delta, cols, val, ws, wn, halo_out, base_v, halo_v, acc_v)
    go.store(base_v, base_out)
    go.finish()


def delta_of(arr, before, slope, row):
    back = return_rows(row[...], arr[...], before.shape[0])
    grad = (before[...] + back).astype(jnp.bfloat16)
    return (grad.astype(jnp.float32) * slope[...]).astype(jnp.bfloat16)


def backward_kernel(
    cols, arr, before, slope, row, val, ws, wn, delta_out, halo_out, base_out,
    delta_v, halo_v, base_v, acc_v, sems,
):
    go = Copies(sems)
    delta = delta_of(arr, before, slope, row)
    delta_v[...] = delta
    go.store(delta_v, delta_out)
    spread_back(go, delta, cols, val, ws, wn, halo_out, base_v, halo_v, acc_v)
    go.store(base_v, base_out)
    go.finish()


def top_kernel(core, hid, agg, arr, before, slope, row, delta_out, keep, give, sems):
    delta = delta_of(arr, before, slope, row)
    delta_out[...] = delta
    products(core[0], hid, agg, delta, (give, keep))


def spread_kernel(
    layer, cols, delta, val, ws, wn, halo_out, base_out, ws_v, wn_v, halo_v, base_v, acc_v, sems
):
    go = Copies(sems)
    first, second = go.start(wn.at[layer], wn_v), go.start(ws.at[layer], ws_v)
    first.wait()
    spread_back(go, delta[...], cols, val, ws_v, wn_v, halo_out, base_v, halo_v, acc_v, second)
    go.store(base_v, base_out)
    go.finish()


def final_kernel(arr, before, row, grad_out, grad_v, sems):
    go = Copies(sems)
    back = return_rows(row[...], arr[...], before.shape[0])
    grad_v[...] = (before[...] + back).astype(jnp.bfloat16)
    go.store(grad_v, grad_out)
    go.finish()


def products(core, hid_v, agg_v, delta, pairs):
    for side, target in ((1 - core, pairs[0]), (core, pairs[1])):
        for n, source in enumerate((hid_v, agg_v)):

            @pl.when(side == n)
            def _(source=source, target=target):
                target[...] = mm_tn(source[...], delta).astype(jnp.bfloat16)


def weight_kernel(core, hid, agg, delta, keep, give, hid_v, agg_v, delta_v, sems):
    go = Copies(sems)
    loads = [go.start(delta, delta_v), go.start(hid, hid_v), go.start(agg, agg_v)]
    for load in loads:
        load.wait()
    products(core[0], hid_v, agg_v, delta_v[...], (give, keep))


def quarters_kernel(chip, keep, got, *outs):
    size = outs[0].shape[0]
    for m, out in enumerate(outs[:-1]):
        at = pl.ds(pl.multiple_of((chip[0] ^ m) * size, size), size)
        total = keep[at, :].astype(jnp.float32) + got[at, :].astype(jnp.float32)
        out[...] = total.astype(jnp.bfloat16)


def add_kernel(scale, *refs):
    total = refs[0][...].astype(jnp.float32)
    for ref in refs[1:-2]:
        total += ref[...].astype(jnp.float32)
    if scale is not None:
        total *= scale
    refs[-2][...] = total.astype(jnp.bfloat16)


def place_kernel(layers, count, where, *refs):
    mine, other = refs[:count], refs[count : 2 * count]
    self_out, neigh_out, sems = refs[-3:]
    size = mine[0].shape[0] // len(layers)
    for core, outs in enumerate(((self_out, neigh_out), (neigh_out, self_out))):

        @pl.when(where[0] == core)
        def _(outs=outs):
            copies = []
            for m, source in enumerate((*mine, *other)):
                to = pl.multiple_of((where[1] ^ (m % count)) * size, size)
                for n, layer in enumerate(layers):
                    copies.append(
                        pltpu.make_async_copy(
                            source.at[pl.ds(n * size, size)],
                            outs[m // count].at[layer, pl.ds(to, size)],
                            sems.at[len(copies)],
                        )
                    )
            for copy in copies:
                copy.start()
            for copy in copies:
                copy.wait()


def per_device(
    features, cotangent, self_weight, neigh_weight, block_val, block_col, send_idx, send_count
):
    outer = lax.axis_size("gx")
    inner = lax.axis_size("gy")
    devices = outer * inner
    nodes, width = features.shape
    tile = block_val.shape[2]
    layers = self_weight.shape[0]
    slots = send_idx.shape[2]
    halo = devices * slots
    ext_tiles = (nodes + halo) // tile
    scale = 1.0 / math.sqrt(nodes * devices)
    bf16, f32, i32 = jnp.bfloat16, jnp.float32, jnp.int32
    near, away, scalars = pltpu.VMEM, pltpu.HBM, pltpu.SMEM

    def call(body, args, outs, scratch=(), sems=None, flops=0, alias=None):
        moved = sum(math.prod(o[0]) * jnp.dtype(o[1]).itemsize for o in outs)
        operands = [
            a if space is scalars else pltpu.with_memory_space_constraint(a, space)
            for a, space in args
        ]
        sems = len(args) + len(outs) if sems is None else sems
        return pl.pallas_call(
            body,
            in_specs=[pl.BlockSpec(memory_space=space) for _, space in args],
            out_specs=[pl.BlockSpec(memory_space=o[2]) for o in outs],
            out_shape=[o[2](o[0], o[1]) for o in outs],
            scratch_shapes=[*(pltpu.VMEM(*s) for s in scratch), pltpu.SemaphoreType.DMA((sems,))],
            input_output_aliases=alias or {},
            cost_estimate=pl.CostEstimate(
                flops=flops, bytes_accessed=2 * moved, transcendentals=0
            ),
            compiler_params=pltpu.CompilerParams(vmem_limit_bytes=16 << 20),
        )(*operands)

    rows, rows32 = ((nodes, width), bf16), ((nodes, width), f32)
    square, halo_rows = ((width, width), bf16), ((halo, width), bf16)
    ext, acc = ((ext_tiles, tile, width), bf16), ((ext_tiles, tile, width), f32)
    big = 8 * nodes * width * width

    def exchange(array):
        sent = array.reshape(devices, slots, width)
        return lax.all_to_all(sent, AXES, 0, 0, tiled=True).reshape(halo, width)

    position = lax.axis_index("gy")
    core, chip = position & 1, position >> 1
    core_arg = core.reshape(1)
    chips = inner // 2
    gx_bits = list(range(outer.bit_length() - 1))

    def flip(array, mask):
        return lax.ppermute(array, "gy", [(j, j ^ mask) for j in range(inner)])

    def flip_to(m, array):
        return flip(array, 2 * m)

    def add(*arrays, scaling=None):
        (total,) = call(
            functools.partial(add_kernel, scaling),
            [(a, near) for a in arrays],
            ((arrays[0].shape, bf16, near),),
        )
        return total

    def chip_sum(keep, give):
        got = flip(give, 1)
        mine, *others = call(
            quarters_kernel,
            ((chip.reshape(1), scalars), (keep, near), (got, near)),
            (((width // chips, width), bf16, near),) * chips,
        )
        total = add(mine, *(flip_to(m, other) for m, other in enumerate(others, 1)))
        for bit in gx_bits:
            perm = [(j, j ^ (1 << bit)) for j in range(outer)]
            got = lax.ppermute(total, "gx", perm)
            total = add(total, got, scaling=scale if bit == gx_bits[-1] else None)
        return total

    def gather(piece):
        mine, other = [piece], []
        for m in range(1, chips):
            mine.append(flip(piece, 2 * m))
        for m in range(chips):
            other.append(flip(mine[m], 1))
        return mine, other

    where = jnp.stack([core, chip]).astype(i32)

    def place(group, mine, other, outs):
        return call(
            functools.partial(place_kernel, group, chips),
            ((where, scalars), *((a, near) for a in (*mine, *other)), *((o, away) for o in outs)),
            ((self_weight.shape, bf16, away),) * 2,
            (),
            2 * chips * len(group),
            alias={1 + 2 * chips: 0, 2 + 2 * chips: 1} if outs else None,
        )

    weights = (self_weight, neigh_weight)

    def load(layer, *arrays):
        return call(
            functools.partial(load_kernel, layer),
            [(a, away) for a in arrays],
            [
                (a.shape[1:] if a is self_weight or a is neigh_weight else a.shape, a.dtype, near)
                for a in arrays
            ],
        )

    cols = (block_col, scalars)
    row, col, send = call(
        first_kernel,
        ((send_idx.transpose(0, 2, 1), away), (send_count, away), (features, away)),
        (((1, halo), i32, near), ((halo, 1), i32, near), (*halo_rows, away)),
        (
            ((1, slots, devices), i32), ((1, devices), i32), rows, halo_rows,
        ),
    )
    arrived = exchange(send)
    ws, wn, hidden, val = load(0, *weights, features, block_val)
    hiddens, aggregates, slopes = [features], [], []
    for layer in range(layers - 1):
        aggregate, slope, kept, hidden, send = call(
            middle_kernel,
            (
                cols, (hidden, near), (arrived, near), (val, near), (ws, near), (wn, near),
                (col, near),
            ),
            ((*rows, away), (*rows32, away), (*rows, away), (*rows, near), (*halo_rows, away)),
            (ext, rows, rows32, halo_rows),
            flops=big,
        )
        hiddens.append(kept)
        aggregates.append(aggregate)
        slopes.append(slope)
        arrived = exchange(send)
        last = layer + 2 == layers
        ws, wn, *cot = load(layer + 1, *weights, *((cotangent,) if last else ()))
    aggregate, delta, outgoing, base = call(
        last_kernel,
        (
            cols, (hidden, near), (arrived, near), (val, near), (ws, near), (wn, near),
            (cot[0], near),
        ),
        ((*rows, away), (*rows, away), (*halo_rows, away), (*rows32, away)),
        (ext, rows, rows, halo_rows, rows32, acc),
        flops=2 * big,
    )
    aggregates.append(aggregate)
    sums = []
    for layer in reversed(range(layers)):
        below = layer - 1
        if layer:
            keep, give = call(
                weight_kernel,
                (
                    (core_arg, scalars), (hiddens[layer], away), (aggregates[layer], away),
                    (delta, away),
                ),
                ((*square, near), (*square, near)),
                (rows, rows, rows),
                flops=big // 2,
            )
        sums.append(chip_sum(keep, give))
        arrived = exchange(outgoing)
        if not layer:
            break
        more = weights if below else (hiddens[0], aggregates[0])
        base, slope, *more = load(below, base, slopes[below], *more)
        back = ((arrived, near), (base, near), (slope, near), (row, near))
        if below:
            delta, outgoing, base = call(
                backward_kernel,
                (cols, *back, (val, near), *((a, near) for a in more)),
                ((*rows, away), (*halo_rows, away), (*rows32, away)),
                (rows, halo_rows, rows32, acc),
                flops=big,
            )
        else:
            delta, keep, give = call(
                top_kernel,
                ((core_arg, scalars), *((a, near) for a in more), *back),
                ((*rows, near), (*square, near), (*square, near)),
                flops=big,
            )
        if not below:
            outgoing, base = call(
                functools.partial(spread_kernel, 0),
                (cols, (delta, near), (val, near), *((w, away) for w in weights)),
                ((*halo_rows, away), (*rows32, away)),
                (square, square, halo_rows, rows32, acc),
                flops=big,
            )
    (base,) = load(0, base)
    (grad,) = call(
        final_kernel, ((arrived, near), (base, near), (row, near)), ((*rows, away),), (rows,)
    )
    outs = ()
    for layer, piece in zip(reversed(range(layers)), sums):
        mine, other = gather(piece)
        outs = place((layer,), mine, other, outs)
    return (*outs, grad)


def solution(mesh):
    return jax.shard_map(
        per_device,
        mesh=mesh,
        in_specs=(
            P(AXES, None),
            P(AXES, None),
            P(),
            P(),
            P(AXES, None, None, None),
            P(AXES, None),
            P(AXES, None, None),
            P(AXES, None),
        ),
        out_specs=(P(), P(), P(AXES, None)),
        check_vma=False,
    )
```

```python
import functools
import math

import jax
import jax.numpy as jnp
from jax import lax
from jax.experimental import pallas as pl
from jax.experimental.pallas import tpu as pltpu
from jax.sharding import PartitionSpec as P


AXES = ("gx", "gy")


def mm(a, b):
    return jnp.dot(a, b, preferred_element_type=jnp.float32)


def mm_tn(a, b):
    return lax.dot_general(a, b, (((0,), (0,)), ((), ())), preferred_element_type=jnp.float32)


def mm_nt(a, b):
    return lax.dot_general(a, b, (((1,), (1,)), ((), ())), preferred_element_type=jnp.float32)


def iota(shape, dim):
    return lax.broadcasted_iota(jnp.int32, shape, dim)


def ones_where(mask):
    return jnp.where(mask, 1.0, 0.0).astype(jnp.bfloat16)


def pick_rows(col, table):
    hot = ones_where(iota((col.shape[0], table.shape[0]), 1) == col)
    return mm(hot, table).astype(jnp.bfloat16)


def return_rows(row, arrived, nodes):
    hot = ones_where(iota((nodes, row.shape[1]), 0) == row)
    return mm(hot, arrived)


class Copies:
    def __init__(self, sems):
        self.sems, self.used, self.stores = sems, 0, []

    def start(self, source, target):
        copy = pltpu.make_async_copy(source, target, self.sems.at[self.used])
        self.used += 1
        copy.start()
        return copy

    def store(self, source, target):
        self.stores.append(self.start(source, target))

    def finish(self):
        for copy in self.stores:
            copy.wait()


def first_kernel(idx, cnt, table, row_out, col_out, send_out, idx_v, cnt_v, table_v, send_v, sems):
    go = Copies(sems)
    loads = [go.start(idx, idx_v), go.start(cnt, cnt_v), go.start(table, table_v)]
    _, slots, peers = idx.shape
    total = peers * slots
    start_t = iota((total, peers), 1) * slots
    place_t = iota((total, peers), 0)
    inside_t = ones_where((place_t >= start_t) & (place_t < start_t + slots))
    here_t = (iota((total, slots), 0) & (slots - 1)) == iota((total, slots), 1)
    loads[0].wait()
    loads[1].wait()
    live = iota((slots, peers), 0) < jnp.broadcast_to(cnt_v[...], (slots, peers))
    code = jnp.where(live, idx_v[0] + 1, 0).astype(jnp.float32).astype(jnp.bfloat16)
    col = jnp.sum(jnp.where(here_t, mm_nt(inside_t, code), 0.0), axis=1, keepdims=True) - 1.0
    col = col.astype(jnp.int32)
    col_out[...] = col
    loads[2].wait()
    send_v[...] = pick_rows(col, table_v[...])
    go.store(send_v, send_out)
    start = iota((peers, total), 0) * slots
    place = iota((peers, total), 1)
    inside = ones_where((place >= start) & (place < start + slots))
    here = (iota((slots, total), 1) & (slots - 1)) == iota((slots, total), 0)
    row = jnp.sum(jnp.where(here, mm(code, inside), 0.0), axis=0, keepdims=True) - 1.0
    row_out[...] = row.astype(jnp.int32)
    go.finish()


def load_kernel(layer, *refs):
    count = (len(refs) - 1) // 2
    go = Copies(refs[-1])
    for source, target in zip(refs[:count], refs[count:-1]):
        go.store(source if source.shape == target.shape else source.at[layer], target)
    go.finish()


def store_kernel(*refs):
    count = (len(refs) - 1) // 2
    go = Copies(refs[-1])
    for source, target in zip(refs[:count], refs[count:-1]):
        go.store(source, target)
    go.finish()


def pre_activation(cols, hid, arr, val, ws, wn, agg_v, ext_v):
    tiles, blocks, tile, _ = val.shape
    own = hid.shape[0] // tile
    for t in range(own):
        ext_v[t] = hid[t * tile : (t + 1) * tile, :]
    for t in range(arr.shape[0] // tile):
        ext_v[own + t] = arr[t * tile : (t + 1) * tile, :]
    for r in range(tiles):
        total = mm(val[r, 0], ext_v[cols[r, 0]])
        for b in range(1, blocks):
            total += mm(val[r, b], ext_v[cols[r, b]])
        agg_v[r * tile : (r + 1) * tile, :] = total.astype(jnp.bfloat16)
    return mm(hid[...], ws[...]) + mm(agg_v[...], wn[...])


def middle_kernel(
    cols, hid, arr, val, ws, wn, col, agg, slope, after, send_out, ext_v, send_v, sems
):
    go = Copies(sems)
    pre = pre_activation(cols, hid, arr, val, ws, wn, agg, ext_v)
    sigma = jax.nn.sigmoid(pre)
    hidden = (pre * sigma).astype(jnp.bfloat16)
    after[...] = hidden
    send_v[...] = pick_rows(col[...], hidden)
    go.store(send_v, send_out)
    slope[...] = sigma * (1.0 + pre * (1.0 - sigma))
    go.finish()


def spread_back(go, delta, cols, val, ws, wn, halo_out, base, halo_v, acc_v, ready=None):
    tiles, blocks, tile, _ = val.shape
    own = base.shape[0] // tile
    acc_v[...] = jnp.zeros_like(acc_v)
    upstream = mm_nt(delta, wn[...]).astype(jnp.bfloat16)
    for r in range(tiles):
        part = upstream[r * tile : (r + 1) * tile, :]
        for b in range(blocks):
            acc_v[cols[r, b]] += mm_tn(val[r, b], part)
    for t in range(halo_out.shape[0] // tile):
        halo_v[t * tile : (t + 1) * tile, :] = acc_v[own + t].astype(jnp.bfloat16)
    go.store(halo_v, halo_out)
    if ready is not None:
        ready.wait()
    own_part = mm_nt(delta, ws[...])
    for t in range(own):
        at = slice(t * tile, (t + 1) * tile)
        base[at, :] = own_part[at, :] + acc_v[t]


def last_kernel(
    cols, hid, arr, val, ws, wn, cot, agg_out, delta_out, halo_out, base,
    ext_v, agg_v, delta_v, halo_v, acc_v, sems,
):
    go = Copies(sems)
    pre = pre_activation(cols, hid, arr, val, ws, wn, agg_v, ext_v)
    go.store(agg_v, agg_out)
    sigma = jax.nn.sigmoid(pre)
    slope = sigma * (1.0 + pre * (1.0 - sigma))
    delta = (cot[...].astype(jnp.float32) * slope).astype(jnp.bfloat16)
    delta_v[...] = delta
    go.store(delta_v, delta_out)
    spread_back(go, delta, cols, val, ws, wn, halo_out, base, halo_v, acc_v)
    go.finish()


def delta_of(arr, before, slope, row):
    back = return_rows(row[...], arr[...], before.shape[0])
    grad = (before[...] + back).astype(jnp.bfloat16)
    return (grad.astype(jnp.float32) * slope[...]).astype(jnp.bfloat16)


def backward_kernel(
    cols, arr, before, slope, row, val, ws, wn, delta_out, halo_out, base,
    delta_v, halo_v, acc_v, sems,
):
    go = Copies(sems)
    delta = delta_of(arr, before, slope, row)
    delta_v[...] = delta
    go.store(delta_v, delta_out)
    spread_back(go, delta, cols, val, ws, wn, halo_out, base, halo_v, acc_v)
    go.finish()


def top_kernel(core, hid, agg, arr, before, slope, row, delta_out, keep, give, sems):
    delta = delta_of(arr, before, slope, row)
    delta_out[...] = delta
    products(core[0], hid, agg, delta, (give, keep))


def spread_kernel(
    layer, cols, delta, val, ws, wn, halo_out, base_out, ws_v, wn_v, halo_v, base_v, acc_v, sems
):
    go = Copies(sems)
    first, second = go.start(wn.at[layer], wn_v), go.start(ws.at[layer], ws_v)
    first.wait()
    spread_back(go, delta[...], cols, val, ws_v, wn_v, halo_out, base_v, halo_v, acc_v, second)
    go.store(base_v, base_out)
    go.finish()


def products(core, hid_v, agg_v, delta, pairs):
    for side, target in ((1 - core, pairs[0]), (core, pairs[1])):
        for n, source in enumerate((hid_v, agg_v)):

            @pl.when(side == n)
            def _(source=source, target=target):
                target[...] = mm_tn(source[...], delta).astype(jnp.bfloat16)


def weight_kernel(core, hid, agg, delta, keep, give, hid_v, agg_v, delta_v, sems):
    go = Copies(sems)
    loads = [go.start(delta, delta_v), go.start(hid, hid_v), go.start(agg, agg_v)]
    for load in loads:
        load.wait()
    products(core[0], hid_v, agg_v, delta_v[...], (give, keep))


def quarters_kernel(chip, keep, got, *outs):
    size = outs[0].shape[0]
    for m, out in enumerate(outs[:-1]):
        at = pl.ds(pl.multiple_of((chip[0] ^ m) * size, size), size)
        total = keep[at, :].astype(jnp.float32) + got[at, :].astype(jnp.float32)
        out[...] = total.astype(jnp.bfloat16)


def add_kernel(scale, *refs):
    total = refs[0][...].astype(jnp.float32)
    for ref in refs[1:-2]:
        total += ref[...].astype(jnp.float32)
    if scale is not None:
        total *= scale
    refs[-2][...] = total.astype(jnp.bfloat16)


def place_copies(layers, count, where, sources, targets, sems, step):
    size = sources[0].shape[0] // len(layers)
    for core in range(2):

        @pl.when(where[0] == core)
        def _(outs=targets if core == 0 else targets[::-1]):
            used = 0
            for m, source in enumerate(sources):
                to = pl.multiple_of((where[1] ^ (m % count)) * size, size)
                for n, layer in enumerate(layers):
                    copy = pltpu.make_async_copy(
                        source.at[pl.ds(n * size, size)],
                        outs[m // count].at[layer, pl.ds(to, size)],
                        sems.at[used],
                    )
                    used += 1
                    getattr(copy, step)()


def place_kernel(layers, count, where, *refs):
    for step in ("start", "wait"):
        place_copies(layers, count, where, refs[: 2 * count], refs[-3:-1], refs[-1], step)


def end_kernel(layers, count, where, *refs):
    ops = 1 + 2 * count
    arr, before, row = refs[ops - 1 : ops + 2]
    self_out, neigh_out, grad, grad_v, sems = refs[-5:]
    source = refs[: 2 * count]
    place_copies(layers, count, where, source, (self_out, neigh_out), sems, "start")
    back = return_rows(row[...], arr[...], before.shape[0])
    grad_v[...] = (before[...] + back).astype(jnp.bfloat16)
    last = pltpu.make_async_copy(grad_v, grad, sems.at[2 * count * len(layers)])
    last.start()
    place_copies(layers, count, where, source, (self_out, neigh_out), sems, "wait")
    last.wait()


def per_device(
    features, cotangent, self_weight, neigh_weight, block_val, block_col, send_idx, send_count
):
    outer = lax.axis_size("gx")
    inner = lax.axis_size("gy")
    devices = outer * inner
    nodes, width = features.shape
    tile = block_val.shape[2]
    layers = self_weight.shape[0]
    slots = send_idx.shape[2]
    halo = devices * slots
    ext_tiles = (nodes + halo) // tile
    scale = 1.0 / math.sqrt(nodes * devices)
    bf16, f32, i32 = jnp.bfloat16, jnp.float32, jnp.int32
    near, away, scalars = pltpu.VMEM, pltpu.HBM, pltpu.SMEM

    def call(body, args, outs, scratch=(), sems=None, flops=0, alias=None):
        moved = sum(math.prod(o[0]) * jnp.dtype(o[1]).itemsize for o in outs)
        operands = [
            a if space is scalars else pltpu.with_memory_space_constraint(a, space)
            for a, space in args
        ]
        sems = len(args) + len(outs) if sems is None else sems
        return pl.pallas_call(
            body,
            in_specs=[pl.BlockSpec(memory_space=space) for _, space in args],
            out_specs=[pl.BlockSpec(memory_space=o[2]) for o in outs],
            out_shape=[o[2](o[0], o[1]) for o in outs],
            scratch_shapes=[*(pltpu.VMEM(*s) for s in scratch), pltpu.SemaphoreType.DMA((sems,))],
            input_output_aliases=alias or {},
            cost_estimate=pl.CostEstimate(
                flops=flops, bytes_accessed=2 * moved, transcendentals=0
            ),
            compiler_params=pltpu.CompilerParams(vmem_limit_bytes=16 << 20),
        )(*operands)

    rows, rows32 = ((nodes, width), bf16), ((nodes, width), f32)
    square, halo_rows = ((width, width), bf16), ((halo, width), bf16)
    ext, acc = ((ext_tiles, tile, width), bf16), ((ext_tiles, tile, width), f32)
    big = 8 * nodes * width * width

    def exchange(array):
        sent = array.reshape(devices, slots, width)
        return lax.all_to_all(sent, AXES, 0, 0, tiled=True).reshape(halo, width)

    position = lax.axis_index("gy")
    core, chip = position & 1, position >> 1
    core_arg = core.reshape(1)
    chips = inner // 2
    gx_bits = list(range(outer.bit_length() - 1))

    def flip(array, mask):
        return lax.ppermute(array, "gy", [(j, j ^ mask) for j in range(inner)])

    def flip_to(m, array):
        return flip(array, 2 * m)

    def add(*arrays, scaling=None):
        (total,) = call(
            functools.partial(add_kernel, scaling),
            [(a, near) for a in arrays],
            ((arrays[0].shape, bf16, near),),
        )
        return total

    def chip_sum(keep, give):
        got = flip(give, 1)
        mine, *others = call(
            quarters_kernel,
            ((chip.reshape(1), scalars), (keep, near), (got, near)),
            (((width // chips, width), bf16, near),) * chips,
        )
        total = add(mine, *(flip_to(m, other) for m, other in enumerate(others, 1)))
        for bit in gx_bits:
            perm = [(j, j ^ (1 << bit)) for j in range(outer)]
            got = lax.ppermute(total, "gx", perm)
            total = add(total, got, scaling=scale if bit == gx_bits[-1] else None)
        return total

    def gather(piece):
        mine, other = [piece], []
        for m in range(1, chips):
            mine.append(flip(piece, 2 * m))
        for m in range(chips):
            other.append(flip(mine[m], 1))
        return mine, other

    where = jnp.stack([core, chip]).astype(i32)

    def place(group, mine, other, outs):
        return call(
            functools.partial(place_kernel, group, chips),
            ((where, scalars), *((a, near) for a in (*mine, *other)), *((o, away) for o in outs)),
            ((self_weight.shape, bf16, away),) * 2,
            (),
            2 * chips * len(group),
            alias={1 + 2 * chips: 0, 2 + 2 * chips: 1} if outs else None,
        )

    weights = (self_weight, neigh_weight)

    def load(layer, *arrays):
        return call(
            functools.partial(load_kernel, layer),
            [(a, away) for a in arrays],
            [
                (a.shape[1:] if a is self_weight or a is neigh_weight else a.shape, a.dtype, near)
                for a in arrays
            ],
        )

    def store(*arrays):
        return call(
            store_kernel, [(a, near) for a in arrays], [(a.shape, a.dtype, away) for a in arrays]
        )

    cols = (block_col, scalars)
    row, col, send = call(
        first_kernel,
        ((send_idx.transpose(0, 2, 1), away), (send_count, away), (features, away)),
        (((1, halo), i32, near), ((halo, 1), i32, near), (*halo_rows, away)),
        (
            ((1, slots, devices), i32), ((1, devices), i32), rows, halo_rows,
        ),
    )
    arrived = exchange(send)
    ws, wn, hidden, val = load(0, *weights, features, block_val)
    hiddens, aggregates, slopes = [features], [], []
    for layer in range(layers - 1):
        aggregate, slope, hidden, send = call(
            middle_kernel,
            (
                cols, (hidden, near), (arrived, near), (val, near), (ws, near), (wn, near),
                (col, near),
            ),
            ((*rows, near), (*rows32, near), (*rows, near), (*halo_rows, away)),
            (ext, halo_rows),
            flops=big,
        )
        arrived = exchange(send)
        aggregate, slope, kept = store(aggregate, slope, hidden)
        hiddens.append(kept)
        aggregates.append(aggregate)
        slopes.append(slope)
        last = layer + 2 == layers
        ws, wn, *cot = load(layer + 1, *weights, *((cotangent,) if last else ()))
    aggregate, delta, outgoing, base = call(
        last_kernel,
        (
            cols, (hidden, near), (arrived, near), (val, near), (ws, near), (wn, near),
            (cot[0], near),
        ),
        ((*rows, away), (*rows, away), (*halo_rows, away), (*rows32, near)),
        (ext, rows, rows, halo_rows, acc),
        flops=2 * big,
    )
    aggregates.append(aggregate)
    sums = []
    for layer in reversed(range(layers)):
        below = layer - 1
        if layer:
            keep, give = call(
                weight_kernel,
                (
                    (core_arg, scalars), (hiddens[layer], away), (aggregates[layer], away),
                    (delta, away),
                ),
                ((*square, near), (*square, near)),
                (rows, rows, rows),
                flops=big // 2,
            )
        sums.append(chip_sum(keep, give))
        arrived = exchange(outgoing)
        if not layer:
            break
        more = weights if below else (hiddens[0], aggregates[0])
        (base,) = store(base)
        base, slope, *more = load(below, base, slopes[below], *more)
        back = ((arrived, near), (base, near), (slope, near), (row, near))
        if below:
            delta, outgoing, base = call(
                backward_kernel,
                (cols, *back, (val, near), *((a, near) for a in more)),
                ((*rows, away), (*halo_rows, away), (*rows32, near)),
                (rows, halo_rows, acc),
                flops=big,
            )
        else:
            delta, keep, give = call(
                top_kernel,
                ((core_arg, scalars), *((a, near) for a in more), *back),
                ((*rows, near), (*square, near), (*square, near)),
                flops=big,
            )
        if not below:
            outgoing, base = call(
                functools.partial(spread_kernel, 0),
                (cols, (delta, near), (val, near), *((w, away) for w in weights)),
                ((*halo_rows, away), (*rows32, away)),
                (square, square, halo_rows, rows32, acc),
                flops=big,
            )
    (base,) = load(0, base)
    outs = ()
    for layer, piece in zip(reversed(range(layers)), sums):
        mine, other = gather(piece)
        if layer:
            outs = place((layer,), mine, other, outs)
        else:
            args = (
                (where, scalars), *((a, near) for a in (*mine, *other)),
                (arrived, near), (base, near), (row, near), *((o, away) for o in outs),
            )
            first = len(args) - len(outs)
            outs = call(
                functools.partial(end_kernel, (0,), chips),
                args,
                (*((self_weight.shape, bf16, away),) * 2, (*rows, away)),
                (rows,),
                2 * chips + 1,
                alias={first: 0, first + 1: 1} if len(outs) else None,
            )
    return tuple(outs)


def solution(mesh):
    return jax.shard_map(
        per_device,
        mesh=mesh,
        in_specs=(
            P(AXES, None),
            P(AXES, None),
            P(),
            P(),
            P(AXES, None, None, None),
            P(AXES, None),
            P(AXES, None, None),
            P(AXES, None),
        ),
        out_specs=(P(), P(), P(AXES, None)),
        check_vma=False,
    )
```
